128 devices in a mesh: gx: 4 (over y), gy: 32 (over x, z, core).
Axes of the slice: x: 4, y: 4, z: 4, core: 2. Of those that a mesh axis runs over, the one named last changes fastest.
Arguments:
- a_blocks: bfloat16 [8192, 8, 9216], P(('gx', 'gy')), may hold values from -2 to 2
- a_cols: int32 [8192, 8], P(('gx', 'gy')), may hold values from 0 to 63
- q_blocks: bfloat16 [8192, 9216], P(('gx', 'gy')), may hold values from -0.625 to 0.625
- part_of: int32 [8192, 8], P(('gx', 'gy')), may hold values from 0 to 63
- part_dest: int32 [8192, 1], P(('gx', 'gy')), may hold values from 0 to 31; in each aligned block of 64 rows (0 to 63, 64 to 127, ...) at most 4 rows name the same one
- part_pos: int32 [8192], P(('gx', 'gy')), may hold values from 0 to 15
- g_level: float32 [3, 9216], replicated, may hold values from -0.625 to 0.625
Outputs:
- coarse_first: float32 [256, 8, 9216], P(('gx', 'gy'))
- coarsest: float32 [256, 8, 9216], P(('gx', 'gy'))
The draws below stay inside these ranges and needn't reach their ends.
Inputs may be any that keep to these rules, and one draw needn't show every extreme that they name: `part_dest`: among the partial blocks of one device at most 4 name the same gy index, and some device's blocks name one index exactly 4 times.
All inputs are finite; a program needn't handle non-finite values.
Results may differ from the reference program's by a relative error of at most 0.0029.
Values sent between devices are 32-bit elements; how exact they have to be, the bound alone decides.
No kernel may reach another device: no remote copies, remote signals or barrier semaphores. Data moves between devices by JAX's collectives and lax.ppermute only.
A program may use at most 128 MiB of HBM per device.

```python
import math
import jax
import jax.numpy as jnp
import numpy as np
from jax import lax

B = 96
R = 64
KA = 8
RC = 2
SC = 8
NP = 64
CAP = 4
FINE = 8192
N_GX = 4
N_GY = 32


def set_ends(drawn, own_key, smallest, top_value):
    longest = drawn.shape.index(max(drawn.shape))
    spots = []
    for shift in (0, 1):
        where = [jax.random.randint(jax.random.fold_in(own_key, axis), (), 0, length) for axis, length in enumerate(drawn.shape)]
        where[longest] = (where[longest] + shift) % drawn.shape[longest]
        spots.append(tuple(where))
    return drawn.at[spots[0]].set(smallest).at[spots[1]].set(top_value)


def levels(rng, shape, cuts, low, largest):
    def one(axis_at, blocks):
        heights = jax.random.uniform(jax.random.fold_in(jax.random.fold_in(rng, 6), axis_at), (blocks,), jnp.float32, low / len(cuts), largest / len(cuts))
        return jnp.repeat(jnp.exp(heights), shape[axis_at] // blocks).reshape((-1,) + (1,) * (len(shape) - axis_at - 1))

    gain = one(*cuts[0])
    for cut in cuts[1:]:
        gain = gain * one(*cut)
    return gain


def shared_out(stream_key, own, number, rows, number_of, top, limit, skew):
    ranking = jax.random.permutation(stream_key, number_of)
    crowded, common = load_shares(number_of, rows * top, limit, skew, True), load_shares(number_of, rows * top, limit, skew, False)
    places = jnp.arange(number_of)

    def named(sizes, offset_by):
        used = int((sizes > 0).sum())
        fixed = max(1, used // 4)
        passed = fixed + (places - fixed + offset_by * (used - fixed)) % max(1, number_of - fixed)
        return jnp.zeros((number_of,), jnp.int32).at[ranking[jnp.where(places < fixed, places, passed)]].set(jnp.asarray(sizes, jnp.int32))

    sizes = jnp.where(number % 4 == 0, named(crowded, number // 4), named(common, number - number // 4 - 1))
    mixed = jax.random.permutation(jax.random.fold_in(own, 3), number_of)
    donor, taker = mixed[0:number_of // 2 * 2:2], mixed[1:number_of // 2 * 2:2]
    slack = jnp.minimum(sizes[donor] - 1, limit - sizes[taker]) // 2
    slack = jnp.where((donor == ranking[0]) | (taker == ranking[0]) | (sizes[taker] == 0), 0, jnp.maximum(slack, 0))
    passed = jax.random.randint(jax.random.fold_in(own, 4), (number_of // 2,), 0, 1 << 20) % (slack + 1)
    sizes = sizes.at[donor].add(-passed).at[taker].add(passed)
    members = jnp.searchsorted(jnp.cumsum(sizes), jnp.arange(rows * top), side="right").astype(jnp.int32)
    table = members.reshape(top, rows).T
    table = table[jax.random.permutation(jax.random.fold_in(own, 1), rows)]
    offset_by = jax.random.randint(jax.random.fold_in(own, 2), (rows, 1), 0, top)
    return jnp.take_along_axis(table, (jnp.arange(top)[None, :] + offset_by) % top, axis=1)


def load_shares(amount, total, bound, lean, full):
    loads = [(1 << 20) // math.isqrt(standing ** lean) + 1 for standing in range(1, amount + 1)]
    largest = bound if full else min(bound, max(-(-total // amount), total * loads[0] // sum(loads)))
    least = 1 if total - largest >= amount - 1 else 0
    holding, surplus = [largest] + [least] * (amount - 1), total - largest - least * (amount - 1)
    while surplus > 0:
        movable = [i for i in range(1, amount) if holding[i] < largest] or [i for i in range(1, amount) if holding[i] < bound]
        whole, left = sum([loads[i] for i in movable]), surplus
        for i in movable:
            extra = min(bound - holding[i], max(1, left * loads[i] // whole), surplus)
            holding[i] = holding[i] + extra
            surplus = surplus - extra
    return np.array(holding)


def bell_draw(stream_key, extent, scale, reach, shards=(), kind=jnp.bfloat16):
    gain = levels(stream_key, extent, shards, -0.22, 0.18) if shards else 1.0
    drawn = jax.random.normal(stream_key, extent, jnp.float32) * scale * gain
    return jnp.minimum(jnp.maximum(drawn, -reach), reach).astype(kind)


def setup_inputs(seed: int = 0) -> dict:
    key_list = jax.random.split(jax.random.key(seed), 8)
    a_blocks = bell_draw(key_list[0], (FINE, KA, B * B), 0.15, 2.0, ((0, 128),))
    a_cols = set_ends(jax.random.randint(key_list[1], (FINE, KA), 0, R), jax.random.fold_in(key_list[1], 1), 0, R - 1).astype(jnp.int32)
    q_blocks = bell_draw(key_list[2], (FINE, B * B), B ** -0.5, 0.625, ((0, 128),))
    part_of = set_ends(jax.random.randint(key_list[3], (FINE, KA), 0, NP), jax.random.fold_in(key_list[3], 1), 0, NP - 1).astype(jnp.int32)
    part_dest_keys = jax.random.split(jax.random.fold_in(key_list[4], 1), (NP * N_GX * N_GY) // NP)
    part_dest_turns = jax.random.permutation(jax.random.fold_in(key_list[4], 3), (NP * N_GX * N_GY) // NP)
    part_dest = jax.vmap(lambda own, number: shared_out(jax.random.fold_in(key_list[4], 2), own, number, NP, N_GY, 1, CAP, 2))(part_dest_keys, part_dest_turns).reshape((NP * N_GX * N_GY, 1))
    part_pos = set_ends(jax.random.randint(key_list[5], (NP * N_GX * N_GY,), 0, RC * SC), jax.random.fold_in(key_list[5], 1), 0, (RC * SC) - 1).astype(jnp.int32)
    g_level = bell_draw(key_list[6], (3, B * B), B ** -0.5, 0.625, (), jnp.float32)
    return {"a_blocks": a_blocks, "a_cols": a_cols, "q_blocks": q_blocks, "part_of": part_of, "part_dest": part_dest, "part_pos": part_pos, "g_level": g_level}


def project(blocks, gmat):
    right = jnp.einsum('...ab,bj->...aj', blocks, gmat, precision=lax.Precision.HIGHEST)
    return jnp.einsum('ai,...aj->...ij', gmat, right, precision=lax.Precision.HIGHEST)


def reference(a_blocks, a_cols, q_blocks, part_of, part_dest, part_pos, g_level):
    ndev = N_GX * N_GY
    cells = RC * SC
    width = B * B
    a_all = a_blocks.reshape(ndev, R, KA, B, B)
    c_all = a_cols.reshape(ndev, R, KA)
    q_all = q_blocks.reshape(ndev, R, B, B)
    p_all = part_of.reshape(ndev, R * KA)
    dst_all = part_dest.reshape(ndev, NP)
    pos_all = part_pos.reshape(ndev, NP)
    ids = jnp.arange(ndev, dtype=jnp.int32)

    def step(carry, items):
        a_dev, c_dev, q_dev, p_dev, dst_dev, pos_dev, dev = items
        qfull = q_dev.astype(jnp.float32)
        picked = qfull[c_dev]
        aq_rows = jnp.einsum('rkij,rkjl->rkil', a_dev.astype(jnp.float32), picked).astype(jnp.bfloat16)
        terms = jnp.einsum('rji,rkjl->rkil', qfull, aq_rows.astype(jnp.float32))
        partial_value = jax.ops.segment_sum(terms.reshape(R * KA, width), p_dev, num_segments=NP)
        target = (((dev // N_GY) * N_GY + dst_dev) * cells + pos_dev).astype(jnp.int32)
        return carry.at[target].add(partial_value), None

    start = jnp.zeros((ndev * cells, width), jnp.float32)
    total, _ = lax.scan(step, start, (a_all, c_all, q_all, p_all, dst_all, pos_all, ids))
    coarse_first = total.reshape(ndev * RC, SC, width)
    gmats = g_level.reshape(3, B, B)
    level = total.reshape(N_GX, N_GY, cells, B, B)
    level = project(level.reshape(N_GX, N_GY // 2, 2, cells, B, B).sum(2), gmats[0])
    level = project(level.reshape(N_GX, N_GY // 4, 2, cells, B, B).sum(2), gmats[1])
    level = project(level.sum(0), gmats[2])
    spread = jnp.broadcast_to(level[None, :, None], (N_GX, N_GY // 4, 4, cells, B, B))
    coarsest = spread.reshape(ndev * RC, SC, width)
    return coarse_first, coarsest
```

```python
import functools
import jax
import jax.numpy as jnp
from jax import lax
from jax.experimental import pallas as pl
from jax.experimental.pallas import tpu as pltpu
from jax.sharding import PartitionSpec as P

B = 96
L = 128
R = 64
KA = 8
RC = 2
SC = 8
NP = 64
CELLS = RC * SC
WIDTH = B * B
GY = 32
GX = 4
PER = B // GY
TILES = 18
ROWS_STEP = 4


def lane_iota(rows):
    return lax.broadcasted_iota(jnp.int32, (rows, L), 1)


def unpack_rows(t0, t1, t2):
    lane = lane_iota(t0.shape[0])
    r1 = jnp.where(lane < 32, pltpu.roll(t0, 32, 1), pltpu.roll(t1, 32, 1))
    r2 = jnp.where(lane < 64, pltpu.roll(t1, 64, 1), pltpu.roll(t2, 64, 1))
    return t0, r1, r2, pltpu.roll(t2, 96, 1)


def pack_rows(v0, v1, v2, v3):
    lane = lane_iota(v0.shape[0])
    s1 = pltpu.roll(v1, 96, 1)
    s2 = pltpu.roll(v2, 64, 1)
    s3 = pltpu.roll(v3, 32, 1)
    return jnp.where(lane < 96, v0, s1), jnp.where(lane < 64, s1, s2), jnp.where(lane < 32, s2, s3)


def fine_kernel(cols, part, dest, pos, me, a_ref, q_ref, x_ref, s_ref, q_mat, q_tr, acc):
    step = pl.program_id(0)

    @pl.when(step == 0)
    def _():
        acc[...] = jnp.zeros_like(acc)
        q_mat[...] = jnp.zeros_like(q_mat)
        low = lane_iota(B) < B
        for g in range(R // 16):
            for j in range(B // 4):
                at = [q_ref[16 * g:16 * g + 16, 384 * j + L * u:384 * j + L * (u + 1)].astype(jnp.float32) for u in range(3)]
                for h in range(2):
                    rows = unpack_rows(*[piece[8 * h:8 * h + 8] for piece in at])
                    for v in range(4):
                        s_ref[h, pl.ds(4 * j + v, 8, stride=B), :] = rows[v]

            def one(k, carry):
                mat = jnp.where(low, s_ref[k // 8, pl.ds(pl.multiple_of((k % 8) * B, 8), B), :], 0.0)
                q_mat[16 * g + k, 0:B, :] = mat.astype(jnp.bfloat16)
                q_tr[16 * g + k] = mat.T[0:B].astype(jnp.bfloat16)
                return carry

            lax.fori_loop(0, 16, one, 0)

    def relayout(ii, slot):
        for j in range(B // 4):
            at = [a_ref[ii, :, 384 * j + L * u:384 * j + L * (u + 1)].astype(jnp.float32) for u in range(3)]
            rows = unpack_rows(*at)
            for v in range(4):
                s_ref[slot, pl.ds(4 * j + v, 8, stride=B), :] = rows[v]

    def multiply(ii, slot):
        i = step * ROWS_STEP + ii
        left = q_tr[i]
        for k in range(0, KA, 2):
            aq = []
            for kk in (k, k + 1):
                mat = s_ref[slot, kk * B:(kk + 1) * B, :].astype(jnp.bfloat16)
                aq.append(jnp.dot(mat, q_mat[cols[i, kk]], preferred_element_type=jnp.float32).astype(jnp.bfloat16))
            term = jnp.dot(left, jnp.concatenate(aq, axis=1), preferred_element_type=jnp.float32)
            for n, kk in enumerate((k, k + 1)):
                p = part[i, kk]
                at = pl.ds(pl.multiple_of(p * B, 8), B)
                acc[at, :] = acc[at, :] + term[:, L * n:L * (n + 1)]

    relayout(0, 0)
    for ii in range(ROWS_STEP):
        if ii + 1 < ROWS_STEP:
            relayout(ii + 1, (ii + 1) % 2)
        multiply(ii, ii % 2)

    @pl.when(step == pl.num_programs(0) - 1)
    def _():
        row = lax.broadcasted_iota(jnp.int32, (8, L), 0)
        lane = lane_iota(8)
        base = (me[0] % 8) * 16
        codes = jnp.zeros((8, L), jnp.float32)
        for p in range(NP):
            code = (dest[p, 0] * CELLS + pos[p]).astype(jnp.float32)
            codes = jnp.where((row == p % 4) & (lane == base + p // 4), code, codes)

        def one(w, carry):
            for a in range(PER):
                rows = [acc[pl.ds(v * B + w * PER + a, 16, stride=4 * B), :] for v in range(4)]
                for u, piece in enumerate(pack_rows(*rows)):
                    for h in range(2):
                        x_ref[w, (2 * a + h) * 3 + u] = piece[8 * h:8 * h + 8]
            x_ref[w, TILES] = codes
            return carry

        lax.fori_loop(0, GY, one, 0)


def fine(a_blocks, a_cols, q_blocks, part_of, part_dest, part_pos, me):
    return pl.pallas_call(
        fine_kernel,
        out_shape=jax.ShapeDtypeStruct((GY, TILES + 1, 8, L), jnp.float32),
        grid_spec=pltpu.PrefetchScalarGridSpec(
            num_scalar_prefetch=5,
            grid=(R // ROWS_STEP,),
            in_specs=[
                pl.BlockSpec((ROWS_STEP, KA, WIDTH), lambda g, *_: (g, 0, 0)),
                pl.BlockSpec((R, WIDTH), lambda g, *_: (0, 0)),
            ],
            out_specs=pl.BlockSpec((GY, TILES + 1, 8, L), lambda g, *_: (0, 0, 0, 0)),
            scratch_shapes=[
                pltpu.VMEM((2, KA * B, L), jnp.float32),
                pltpu.VMEM((R, L, L), jnp.bfloat16),
                pltpu.VMEM((R, B, B), jnp.bfloat16),
                pltpu.VMEM((NP * B, L), jnp.float32),
            ],
        ),
        name="fine",
    )(a_cols, part_of, part_dest, part_pos, me, a_blocks, q_blocks)


def split2(x):
    hi = x.astype(jnp.bfloat16)
    return hi, (x - hi.astype(jnp.float32)).astype(jnp.bfloat16)


def cells_kernel(y_ref, z_ref, t_ref, hi_ref, lo_ref):
    def one(s, carry):
        for a in range(PER):
            halves = [unpack_rows(*[y_ref[s, (2 * a + h) * 3 + u] for u in range(3)]) for h in range(2)]
            for v in range(4):
                hi, lo = split2(jnp.concatenate([halves[0][v], halves[1][v]], axis=0))
                at = pl.ds(pl.multiple_of(v * 512 + s * 16, 16), 16)
                hi_ref[at, L * a:L * (a + 1)] = hi
                lo_ref[at, L * a:L * (a + 1)] = lo
        return carry

    lax.fori_loop(0, GY, one, 0)
    tiles = [functools.reduce(jnp.add, [y_ref[8 * o + s, TILES] for s in range(8)]) for o in range(4)]
    codes = jnp.concatenate([tiles[o][v:v + 1] for v in range(4) for o in range(4)], axis=1)

    def chunk(c, carry):
        want = (lax.broadcasted_iota(jnp.int32, (L, 1), 0) + c * L).astype(jnp.float32)
        table = jnp.where(want == codes, 1.0, 0.0).astype(jnp.bfloat16)
        sums = jnp.dot(table, hi_ref[...], preferred_element_type=jnp.float32)
        sums = sums + jnp.dot(table, lo_ref[...], preferred_element_type=jnp.float32)
        for a in range(PER):
            at = sums[:, L * a:L * (a + 1)].reshape(8, 2, 8, L)
            z_ref[pl.ds(c * 8, 8), 2 * a:2 * a + 2] = at
            t_ref[pl.ds(c * 2, 2), 2 * a:2 * a + 2] = at.reshape(2, 4, 2, 8, L).sum(1)
        return carry

    lax.fori_loop(0, 4, chunk, 0)


def cells_of(received):
    return pl.pallas_call(
        cells_kernel,
        out_shape=(
            jax.ShapeDtypeStruct((GY, 2 * PER, 8, L), jnp.float32),
            jax.ShapeDtypeStruct((GY // 4, 2 * PER, 8, L), jnp.float32),
        ),
        scratch_shapes=[pltpu.VMEM((4 * 512, PER * L), jnp.bfloat16)] * 2,
        name="cells",
    )(received)


def close_kernel(w_ref, h_ref, ht_ref, first_ref, last_ref, r_ref, o_ref):
    def rows_of(tile):
        for j in range(B // 4):
            for half in range(RC):
                yield j, half, [tile(4 * j + v, half) for v in range(4)]

    for j, half, rows in rows_of(lambda r, half: w_ref[r // PER, 2 * (r % PER) + half]):
        for u, piece in enumerate(pack_rows(*rows)):
            first_ref[half, :, 384 * j + L * u:384 * j + L * (u + 1)] = piece
    total = w_ref[:, 2 * PER:4 * PER].reshape(B * CELLS, L)
    r_ref[...] = jnp.dot(total, h_ref[...], precision=lax.Precision.HIGHEST, preferred_element_type=jnp.float32)
    for c in range(0, CELLS, 2):
        pair = jnp.concatenate([r_ref[pl.ds(c + n, B, stride=CELLS), :] for n in range(2)], axis=1)
        out = jnp.dot(ht_ref[...], pair, precision=lax.Precision.HIGHEST, preferred_element_type=jnp.float32)
        for n in range(2):
            o_ref[pl.ds(c + n, B, stride=CELLS), :] = out[:, L * n:L * (n + 1)]
    for j, half, rows in rows_of(lambda r, half: o_ref[r * CELLS + 8 * half:r * CELLS + 8 * half + 8, :]):
        for u, piece in enumerate(pack_rows(*rows)):
            last_ref[half, :, 384 * j + L * u:384 * j + L * (u + 1)] = piece


def close(received, h, ht):
    out = jax.ShapeDtypeStruct((RC, SC, WIDTH), jnp.float32)
    return pl.pallas_call(
        close_kernel,
        out_shape=(out, out),
        scratch_shapes=[pltpu.VMEM((B * CELLS, L), jnp.float32)] * 2,
        name="close",
    )(received, h, ht)


def local(a_blocks, a_cols, q_blocks, part_of, part_dest, part_pos, g_level):
    me = lax.axis_index("gy").astype(jnp.int32).reshape(1)
    g = g_level.reshape(3, B, B)
    mm = functools.partial(jnp.dot, precision=lax.Precision.HIGHEST)
    h = mm(mm(g[0], g[1]), g[2])
    slices = fine(a_blocks, a_cols, q_blocks, part_of, part_dest, part_pos, me)
    gathered = lax.all_to_all(slices, "gy", split_axis=0, concat_axis=0, tiled=True)
    mine, group = cells_of(gathered)
    others = [lax.ppermute(group, "gx", [(i, (i + d) % GX) for i in range(GX)]) for d in range(1, GX)]
    total = group + others[0] + others[1] + others[2]
    total = jnp.broadcast_to(total[:, None], (GY // 4, 4) + total.shape[1:]).reshape(mine.shape)
    back = lax.all_to_all(jnp.concatenate([mine, total], axis=1), "gy", split_axis=0, concat_axis=0, tiled=True)
    return close(back, jnp.pad(h, ((0, L - B), (0, L - B))), h.T)


def solution(mesh):
    placed = (
        P(("gx", "gy"), None, None),
        P(("gx", "gy"), None),
        P(("gx", "gy"), None),
        P(("gx", "gy"), None),
        P(("gx", "gy"), None),
        P(("gx", "gy")),
        P(),
    )
    return jax.shard_map(
        local,
        mesh=mesh,
        in_specs=placed,
        out_specs=(P(("gx", "gy"), None, None), P(("gx", "gy"), None, None)),
        check_vma=False,
    )
```

```python
import functools
import jax
import jax.numpy as jnp
from jax import lax
from jax.experimental import pallas as pl
from jax.experimental.pallas import tpu as pltpu
from jax.sharding import PartitionSpec as P

B = 96
L = 128
R = 64
KA = 8
RC = 2
SC = 8
NP = 64
CELLS = RC * SC
WIDTH = B * B
GY = 32
GX = 4
PER = B // GY
TILES = 18
ROWS_STEP = 8
SKEW = 4
STRIDE = 100
APART = 104


def lane_iota(rows):
    return lax.broadcasted_iota(jnp.int32, (rows, L), 1)


def unpack_rows(t0, t1, t2):
    lane = lane_iota(t0.shape[0])
    r1 = jnp.where(lane < 32, pltpu.roll(t0, 32, 1), pltpu.roll(t1, 32, 1))
    r2 = jnp.where(lane < 64, pltpu.roll(t1, 64, 1), pltpu.roll(t2, 64, 1))
    return t0, r1, r2, pltpu.roll(t2, 96, 1)


def pack_rows(v0, v1, v2, v3):
    lane = lane_iota(v0.shape[0])
    s1 = pltpu.roll(v1, 96, 1)
    s2 = pltpu.roll(v2, 64, 1)
    s3 = pltpu.roll(v3, 32, 1)
    return jnp.where(lane < 96, v0, s1), jnp.where(lane < 64, s1, s2), jnp.where(lane < 32, s2, s3)


def fine_kernel(pairs, code, me, a_ref, q_ref, x_ref, s_ref, q_mat, q_tr, acc):
    step = pl.program_id(0)

    def relayout(load, slot, triples):
        for j in triples:
            rows = unpack_rows(*[load(slice(384 * j + L * u, 384 * j + L * (u + 1))).astype(jnp.float32) for u in range(3)])
            for v in range(4):
                s_ref[slot, pl.ds(4 * j + v, 8, stride=STRIDE), :] = rows[v]

    @pl.when(step == 0)
    def _():
        acc[...] = jnp.zeros_like(acc)
        low = lane_iota(B) < B
        unit = (lane_iota(B) == lax.broadcasted_iota(jnp.int32, (B, L), 0)).astype(jnp.bfloat16)

        def group(g, carry):
            both = pl.ds(pl.multiple_of(16 * g, 16), 16)
            for h in range(2):
                relayout(lambda lanes: q_ref[both, lanes][8 * h:8 * h + 8], h, range(B // 4))
            for k in range(16):
                at = (k % 8) * STRIDE
                mat = jnp.where(low, s_ref[k // 8, at:at + B, :], 0.0).astype(jnp.bfloat16)
                q_mat[16 * g + k, 0:B, :] = mat
                q_mat[16 * g + k, B:L, :] = jnp.zeros((L - B, L), jnp.bfloat16)
                turned = lax.dot_general(unit, mat, (((1,), (1,)), ((), ())), preferred_element_type=jnp.float32)
                q_tr[16 * g + k] = turned.astype(jnp.bfloat16)
            return carry

        lax.fori_loop(0, R // 16, group, 0)

    def first(n):
        ii, k = n // 4, 2 * (n % 4)
        aq = []
        for kk in (k, k + 1):
            mat = s_ref[ii % 2, kk * STRIDE:kk * STRIDE + B, :].astype(jnp.bfloat16)
            at = pairs[step * ROWS_STEP + ii, kk] % R
            aq.append(jnp.dot(mat, q_mat[at], preferred_element_type=jnp.float32).astype(jnp.bfloat16))
        return jnp.concatenate(aq, axis=1)

    def second(n, aq):
        ii, k = n // 4, 2 * (n % 4)
        i = step * ROWS_STEP + ii
        term = jnp.dot(q_tr[i], aq, preferred_element_type=jnp.float32)
        for m in range(2):
            p = pairs[i, k + m] // R
            at = pl.ds(pl.multiple_of(p * APART, 8), B)
            acc[at, :] = acc[at, :] + term[:, L * m:L * (m + 1)]

    def prepare(ii, triples):
        relayout(lambda lanes: a_ref[ii, :, lanes], ii % 2, triples)

    prepare(0, range(B // 4))
    held = []
    for n in range(4 * ROWS_STEP + SKEW):
        if n < 4 * ROWS_STEP:
            held.append(first(n))
            if n // 4 + 1 < ROWS_STEP:
                prepare(n // 4 + 1, range(6 * (n % 4), 6 * (n % 4) + 6))
        if n >= SKEW:
            second(n - SKEW, held[n - SKEW])

    @pl.when(step == pl.num_programs(0) - 1)
    def _():
        row = lax.broadcasted_iota(jnp.int32, (8, L), 0)
        lane = lane_iota(8)
        base = (me[0] % 8) * 16
        codes = jnp.zeros((8, L), jnp.float32)
        for p in range(NP):
            codes = jnp.where((row == p // 16) & (lane == base + p % 16), code[p].astype(jnp.float32), codes)

        def one(w, carry):
            for a in range(PER):
                rows = [acc[pl.ds(v * 16 * APART + w * PER + a, 16, stride=APART), :] for v in range(4)]
                for u, piece in enumerate(pack_rows(*rows)):
                    for h in range(2):
                        x_ref[w, (2 * a + h) * 3 + u] = piece[8 * h:8 * h + 8]
            x_ref[w, TILES] = codes
            return carry

        lax.fori_loop(0, GY, one, 0)


def fine(a_blocks, a_cols, q_blocks, part_of, part_dest, part_pos, me):
    pairs = a_cols + R * part_of
    code = part_dest[:, 0] * CELLS + part_pos
    return pl.pallas_call(
        fine_kernel,
        out_shape=jax.ShapeDtypeStruct((GY, TILES + 1, 8, L), jnp.float32),
        grid_spec=pltpu.PrefetchScalarGridSpec(
            num_scalar_prefetch=3,
            grid=(R // ROWS_STEP,),
            in_specs=[
                pl.BlockSpec((ROWS_STEP, KA, WIDTH), lambda g, *_: (g, 0, 0)),
                pl.BlockSpec((R, WIDTH), lambda g, *_: (0, 0)),
            ],
            out_specs=pl.BlockSpec((GY, TILES + 1, 8, L), lambda g, *_: (0, 0, 0, 0)),
            scratch_shapes=[
                pltpu.VMEM((2, KA * STRIDE, L), jnp.float32),
                pltpu.VMEM((R, L, L), jnp.bfloat16),
                pltpu.VMEM((R, B, B), jnp.bfloat16),
                pltpu.VMEM((NP * APART, L), jnp.float32),
            ],
        ),
        name="fine",
    )(pairs, code, me, a_blocks, q_blocks)


def split2(x):
    hi = x.astype(jnp.bfloat16)
    return hi, (x - hi.astype(jnp.float32)).astype(jnp.bfloat16)


def cells_kernel(y_ref, z_ref, t_ref, hi_ref, lo_ref):
    def one(s, carry):
        for a in range(PER):
            halves = [unpack_rows(*[y_ref[s, (2 * a + h) * 3 + u] for u in range(3)]) for h in range(2)]
            for v in range(4):
                hi, lo = split2(jnp.concatenate([halves[0][v], halves[1][v]], axis=0))
                at = pl.ds(pl.multiple_of(v * 512 + s * 16, 16), 16)
                hi_ref[at, L * a:L * (a + 1)] = hi
                lo_ref[at, L * a:L * (a + 1)] = lo
        return carry

    lax.fori_loop(0, GY, one, 0)
    tiles = [functools.reduce(jnp.add, [y_ref[8 * o + s, TILES] for s in range(8)]) for o in range(4)]
    codes = jnp.concatenate([tiles[o][v:v + 1] for v in range(4) for o in range(4)], axis=1)

    def chunk(c, carry):
        want = (lax.broadcasted_iota(jnp.int32, (L, 1), 0) + c * L).astype(jnp.float32)
        table = jnp.where(want == codes, 1.0, 0.0).astype(jnp.bfloat16)
        sums = jnp.dot(table, hi_ref[...], preferred_element_type=jnp.float32)
        sums = sums + jnp.dot(table, lo_ref[...], preferred_element_type=jnp.float32)
        for a in range(PER):
            at = sums[:, L * a:L * (a + 1)].reshape(8, 2, 8, L)
            z_ref[pl.ds(c * 8, 8), 2 * a:2 * a + 2] = at
            t_ref[pl.ds(c * 2, 2), 2 * a:2 * a + 2] = at.reshape(2, 4, 2, 8, L).sum(1)
        return carry

    lax.fori_loop(0, 4, chunk, 0)


def cells_of(received):
    return pl.pallas_call(
        cells_kernel,
        out_shape=(
            jax.ShapeDtypeStruct((GY, 2 * PER, 8, L), jnp.float32),
            jax.ShapeDtypeStruct((GY // 4, 2 * PER, 8, L), jnp.float32),
        ),
        scratch_shapes=[pltpu.VMEM((4 * 512, PER * L), jnp.bfloat16)] * 2,
        name="cells",
    )(received)


def close_kernel(w_ref, h_ref, ht_ref, first_ref, last_ref, r_ref, o_ref):
    def rows_of(tile):
        for j in range(B // 4):
            for half in range(RC):
                yield j, half, [tile(4 * j + v, half) for v in range(4)]

    for j, half, rows in rows_of(lambda r, half: w_ref[r // PER, 2 * (r % PER) + half]):
        for u, piece in enumerate(pack_rows(*rows)):
            first_ref[half, :, 384 * j + L * u:384 * j + L * (u + 1)] = piece
    total = w_ref[:, 2 * PER:4 * PER].reshape(B * CELLS, L)
    r_ref[...] = jnp.dot(total, h_ref[...], precision=lax.Precision.HIGHEST, preferred_element_type=jnp.float32)
    for c in range(0, CELLS, 2):
        pair = jnp.concatenate([r_ref[pl.ds(c + n, B, stride=CELLS), :] for n in range(2)], axis=1)
        out = jnp.dot(ht_ref[...], pair, precision=lax.Precision.HIGHEST, preferred_element_type=jnp.float32)
        for n in range(2):
            o_ref[pl.ds(c + n, B, stride=CELLS), :] = out[:, L * n:L * (n + 1)]
    for j, half, rows in rows_of(lambda r, half: o_ref[r * CELLS + 8 * half:r * CELLS + 8 * half + 8, :]):
        for u, piece in enumerate(pack_rows(*rows)):
            last_ref[half, :, 384 * j + L * u:384 * j + L * (u + 1)] = piece


def close(received, h, ht):
    out = jax.ShapeDtypeStruct((RC, SC, WIDTH), jnp.float32)
    return pl.pallas_call(
        close_kernel,
        out_shape=(out, out),
        scratch_shapes=[pltpu.VMEM((B * CELLS, L), jnp.float32)] * 2,
        name="close",
    )(received, h, ht)


def local(a_blocks, a_cols, q_blocks, part_of, part_dest, part_pos, g_level):
    me = lax.axis_index("gy").astype(jnp.int32).reshape(1)
    g = g_level.reshape(3, B, B)
    mm = functools.partial(jnp.dot, precision=lax.Precision.HIGHEST)
    h = mm(mm(g[0], g[1]), g[2])
    slices = fine(a_blocks, a_cols, q_blocks, part_of, part_dest, part_pos, me)
    gathered = lax.all_to_all(slices, "gy", split_axis=0, concat_axis=0, tiled=True)
    mine, group = cells_of(gathered)
    others = [lax.ppermute(group, "gx", [(i, (i + d) % GX) for i in range(GX)]) for d in range(1, GX)]
    total = group + others[0] + others[1] + others[2]
    total = jnp.broadcast_to(total[:, None], (GY // 4, 4) + total.shape[1:]).reshape(mine.shape)
    back = lax.all_to_all(jnp.concatenate([mine, total], axis=1), "gy", split_axis=0, concat_axis=0, tiled=True)
    return close(back, jnp.pad(h, ((0, L - B), (0, L - B))), h.T)


def solution(mesh):
    placed = (
        P(("gx", "gy"), None, None),
        P(("gx", "gy"), None),
        P(("gx", "gy"), None),
        P(("gx", "gy"), None),
        P(("gx", "gy"), None),
        P(("gx", "gy")),
        P(),
    )
    return jax.shard_map(
        local,
        mesh=mesh,
        in_specs=placed,
        out_specs=(P(("gx", "gy"), None, None), P(("gx", "gy"), None, None)),
        check_vma=False,
    )
```

```python
import functools
import jax
import jax.numpy as jnp
from jax import lax
from jax.experimental import pallas as pl
from jax.experimental.pallas import tpu as pltpu
from jax.sharding import PartitionSpec as P

B = 96
L = 128
R = 64
KA = 8
RC = 2
SC = 8
NP = 64
CELLS = RC * SC
WIDTH = B * B
GY = 32
GX = 4
PER = B // GY
TILES = 18
ROWS_STEP = 8
SKEW = 8
STRIDE = 100
GAP = 20
M_ROWS = 512
APART = 104


def lane_iota(rows):
    return lax.broadcasted_iota(jnp.int32, (rows, L), 1)


def unpack_rows(t0, t1, t2):
    lane = lane_iota(t0.shape[0])
    r1 = jnp.where(lane < 32, pltpu.roll(t0, 32, 1), pltpu.roll(t1, 32, 1))
    r2 = jnp.where(lane < 64, pltpu.roll(t1, 64, 1), pltpu.roll(t2, 64, 1))
    return t0, r1, r2, pltpu.roll(t2, 96, 1)


def pack_rows(v0, v1, v2, v3):
    lane = lane_iota(v0.shape[0])
    s1 = pltpu.roll(v1, 96, 1)
    s2 = pltpu.roll(v2, 64, 1)
    s3 = pltpu.roll(v3, 32, 1)
    return jnp.where(lane < 96, v0, s1), jnp.where(lane < 64, s1, s2), jnp.where(lane < 32, s2, s3)


def fine_kernel(pairs, code, me, a_ref, q_ref, x_ref, s_ref, q_mat, q_tr, acc):
    step = pl.program_id(0)

    def relayout(load, slot, triples):
        for j in triples:
            rows = unpack_rows(*[load(slice(384 * j + L * u, 384 * j + L * (u + 1))).astype(jnp.float32) for u in range(3)])
            for v in range(4):
                s_ref[slot, pl.ds(4 * j + v, 8, stride=STRIDE), :] = rows[v]

    @pl.when(step == 0)
    def _():
        low = lane_iota(B) < B
        unit = (lane_iota(B) == lax.broadcasted_iota(jnp.int32, (B, L), 0)).astype(jnp.bfloat16)
        part_rows = NP * APART // R

        def spread(g, triples):
            both = slice(16 * (g // 2), 16 * (g // 2) + 16)
            relayout(lambda lanes: q_ref[both, lanes][8 * (g % 2):8 * (g % 2) + 8], g % 2, triples)

        spread(0, range(B // 4))
        for c in range(R):
            g, k = divmod(c, 8)
            if c + 8 < R:
                spread(g + 1, range(3 * k, 3 * k + 3))
            acc[c * part_rows:(c + 1) * part_rows, :] = jnp.zeros((part_rows, L), jnp.float32)
            mat = jnp.where(low, s_ref[g % 2, k * STRIDE:k * STRIDE + B, :], 0.0).astype(jnp.bfloat16)
            q_mat[c] = mat
            turned = lax.dot_general(unit, mat, (((1,), (1,)), ((), ())), preferred_element_type=jnp.float32)
            q_tr[c] = turned.astype(jnp.bfloat16)

    def first(n):
        ii, k = n // 4, 2 * (n % 4)
        aq = []
        for kk in (k, k + 1):
            mat = s_ref[ii % 2, kk * STRIDE:kk * STRIDE + B, :].astype(jnp.bfloat16)
            at = pairs[step * ROWS_STEP + ii, kk] % R
            aq.append(jnp.dot(mat[:, :B], q_mat[at], preferred_element_type=jnp.float32).astype(jnp.bfloat16))
        return jnp.concatenate(aq, axis=1)

    def second(n, aq):
        ii, k = n // 4, 2 * (n % 4)
        i = step * ROWS_STEP + ii
        term = jnp.dot(q_tr[i], aq, preferred_element_type=jnp.float32)
        for m in range(2):
            p = pairs[i, k + m] // R
            at = pl.ds(pl.multiple_of(p * APART, 8), B)
            acc[at, :] = acc[at, :] + term[:, L * m:L * (m + 1)]

    def prepare(ii, triples):
        relayout(lambda lanes: a_ref[ii, :, lanes], ii % 2, triples)

    prepare(0, range(B // 4))
    held = []
    for n in range(4 * ROWS_STEP + SKEW):
        if n < 4 * ROWS_STEP:
            held.append(first(n))
            if n // 4 + 1 < ROWS_STEP:
                prepare(n // 4 + 1, range(6 * (n % 4), 6 * (n % 4) + 6))
        if n >= SKEW:
            second(n - SKEW, held[n - SKEW])

    @pl.when(step == pl.num_programs(0) - 1)
    def _():
        row = lax.broadcasted_iota(jnp.int32, (8, L), 0)
        lane = lane_iota(8)
        base = (me[0] % 8) * 16
        codes = jnp.zeros((8, L), jnp.float32)
        for p in range(NP):
            codes = jnp.where((row == p // 16) & (lane == base + p % 16), code[p].astype(jnp.float32), codes)

        def one(w, carry):
            for a in range(PER):
                rows = [acc[pl.ds(v * 16 * APART + w * PER + a, 16, stride=APART), :] for v in range(4)]
                for u, piece in enumerate(pack_rows(*rows)):
                    for h in range(2):
                        x_ref[w, (2 * a + h) * 3 + u] = piece[8 * h:8 * h + 8]
            x_ref[w, TILES] = codes
            return carry

        lax.fori_loop(0, GY, one, 0, unroll=4)


def fine(a_blocks, a_cols, q_blocks, part_of, part_dest, part_pos, me):
    pairs = a_cols + R * part_of
    code = part_dest[:, 0] * CELLS + part_pos
    return pl.pallas_call(
        fine_kernel,
        out_shape=jax.ShapeDtypeStruct((GY, TILES + 1, 8, L), jnp.float32),
        grid_spec=pltpu.PrefetchScalarGridSpec(
            num_scalar_prefetch=3,
            grid=(R // ROWS_STEP,),
            in_specs=[
                pl.BlockSpec((ROWS_STEP, KA, WIDTH), lambda g, *_: (g, 0, 0)),
                pl.BlockSpec((R, WIDTH), lambda g, *_: (0, 0)),
            ],
            out_specs=pl.BlockSpec((GY, TILES + 1, 8, L), lambda g, *_: (0, 0, 0, 0)),
            scratch_shapes=[
                pltpu.VMEM((2, KA * STRIDE, L), jnp.float32),
                pltpu.VMEM((R, B, L), jnp.bfloat16),
                pltpu.VMEM((R, B, B), jnp.bfloat16),
                pltpu.VMEM((NP * APART, L), jnp.float32),
            ],
        ),
        compiler_params=pltpu.CompilerParams(vmem_limit_bytes=58 << 20),
        name="fine",
    )(pairs, code, me, a_blocks, q_blocks)


def split2(x):
    hi = x.astype(jnp.bfloat16)
    return hi, (x - hi.astype(jnp.float32)).astype(jnp.bfloat16)


def cells_kernel(y_ref, z_ref, t_ref, x_ref, m_ref, g_ref):
    wide = 2 * PER * L

    def one(s, carry):
        for a in range(PER):
            halves = [unpack_rows(*[y_ref[s, (2 * a + h) * 3 + u] for u in range(3)]) for h in range(2)]
            for v in range(4):
                hi, lo = split2(jnp.concatenate([halves[0][v], halves[1][v]], axis=0))
                at = pl.ds(pl.multiple_of(v * 512 + s * 16, 16), 16)
                x_ref[at, L * a:L * (a + 1)] = hi
                x_ref[at, L * (PER + a):L * (PER + a + 1)] = lo
        return carry

    lax.fori_loop(0, GY, one, 0, unroll=4)
    tiles = [functools.reduce(jnp.add, [y_ref[8 * o + s, TILES] for s in range(8)]) for o in range(4)]
    codes = jnp.concatenate([tiles[o][v:v + 1] for v in range(4) for o in range(4)], axis=1) - 256.0
    names = codes.astype(jnp.bfloat16)
    row = lax.broadcasted_iota(jnp.int32, (4 * L, 1), 0)
    want = ((row % L) // 4) * CELLS + 4 * (row // L) + row % 4
    want = (want.astype(jnp.float32) - 256.0).astype(jnp.bfloat16)
    one_bf, zero_bf = jnp.ones((), jnp.bfloat16), jnp.zeros((), jnp.bfloat16)
    for c in range(0, 4 * L, M_ROWS):
        table = jnp.where(want[c:c + M_ROWS] == names, one_bf, zero_bf)
        sums = jnp.dot(table, x_ref[...], preferred_element_type=jnp.float32)
        m_ref[c:c + M_ROWS, :] = sums[:, :wide // 2] + sums[:, wide // 2:]

    def fold(g, carry):
        for a in range(PER):
            for v in range(4):
                at = pl.multiple_of(L * v + 16 * g, 16)
                both = m_ref[pl.ds(at, 8), L * a:L * (a + 1)] + m_ref[pl.ds(at + 8, 8), L * a:L * (a + 1)]
                both = both + pltpu.roll(both, 4, 0)
                g_ref[a, v, pl.ds(pl.multiple_of(4 * g, 4), 4), :] = both[0:4]
        return carry

    lax.fori_loop(0, GY // 4, fold, 0, unroll=2)
    for a in range(PER):
        for u, piece in enumerate(pack_rows(*[g_ref[a, v] for v in range(4)])):
            t_ref[3 * a + u] = piece

    def pack(n, carry):
        for a in range(PER):
            rows = [m_ref[pl.ds(pl.multiple_of(L * v + 16 * n, 16), 16), L * a:L * (a + 1)] for v in range(4)]
            for u, piece in enumerate(pack_rows(*rows)):
                z_ref[3 * a + u, pl.ds(pl.multiple_of(16 * n, 16), 16), :] = piece
        return carry

    lax.fori_loop(0, L // 16, pack, 0, unroll=2)


def cells_of(received):
    return pl.pallas_call(
        cells_kernel,
        out_shape=(
            jax.ShapeDtypeStruct((3 * PER, L + 8, L), jnp.float32),
            jax.ShapeDtypeStruct((3 * PER, L // 4, L), jnp.float32),
        ),
        scratch_shapes=[
            pltpu.VMEM((4 * 512, 2 * PER * L), jnp.bfloat16),
            pltpu.VMEM((4 * L, PER * L), jnp.float32),
            pltpu.VMEM((PER, 4, L // 4, L), jnp.float32),
        ],
        compiler_params=pltpu.CompilerParams(vmem_limit_bytes=24 << 20),
        name="cells",
    )(received)


def merge_kernel(z_ref, t0, t1, t2, t3, out_ref, s_ref):
    upper = lax.broadcasted_iota(jnp.int32, (8, L), 0) < 4
    for n in range(3 * PER):
        s_ref[n, 4:L // 4 + 4, :] = (t0[n] + t1[n]) + (t2[n] + t3[n])
    for d in range(GY):
        g = d // 4
        for n in range(3 * PER):
            out_ref[d, n] = jnp.where(upper, z_ref[n, 4 * d:4 * d + 8, :], s_ref[n, 4 * g:4 * g + 8, :])


def merge(mine, parts):
    return pl.pallas_call(
        merge_kernel,
        out_shape=jax.ShapeDtypeStruct((GY, 3 * PER, 8, L), jnp.float32),
        scratch_shapes=[pltpu.VMEM((3 * PER, L // 4 + 8, L), jnp.float32)],
        compiler_params=pltpu.CompilerParams(vmem_limit_bytes=8 << 20),
        name="merge",
    )(mine, *parts)


def close_kernel(w_ref, h_ref, ht_ref, first_ref, last_ref, f_ref, hi_ref, lo_ref, r_ref, o_ref):
    upper = lax.broadcasted_iota(jnp.int32, (8, L), 0) < 4

    def spread(w, carry):
        for a in range(PER):
            rows = unpack_rows(*[w_ref[w, 3 * a + u] for u in range(3)])
            for v in range(4):
                f_ref[v, pl.ds(pl.multiple_of((w * PER + a) * 8 + 8, 8), 8), :] = rows[v]
        return carry

    lax.fori_loop(0, GY, spread, 0, unroll=4)

    def outputs(j, carry):
        lanes = [pl.ds(pl.multiple_of(384 * j + L * u, L), L) for u in range(3)]
        base = pl.multiple_of(32 * j + 8, 8)
        for half in range(RC):
            rows = [jnp.where(upper, f_ref[2 * half, pl.ds(base + 8 * v, 8), :], f_ref[2 * half + 1, pl.ds(base + 8 * v - 4, 8), :]) for v in range(4)]
            for u, piece in enumerate(pack_rows(*rows)):
                first_ref[half, :, lanes[u]] = piece
        for v in range(4):
            both = [jnp.where(upper, f_ref[2 * half, pl.ds(base + 8 * v + 4, 8), :], f_ref[2 * half + 1, pl.ds(base + 8 * v, 8), :]) for half in range(RC)]
            hi, lo = split2(jnp.concatenate(both, axis=0))
            at = pl.ds(pl.multiple_of(64 * j + 16 * v, 16), 16)
            hi_ref[at, :] = hi
            lo_ref[at, :] = lo
        return carry

    lax.fori_loop(0, B // 4, outputs, 0, unroll=2)
    h_hi, h_lo = split2(h_ref[...])
    t_hi, t_lo = split2(ht_ref[...])
    dot = functools.partial(jnp.dot, preferred_element_type=jnp.float32)
    for c in range(0, B, 16):
        at = slice(c * CELLS, (c + 16) * CELLS)
        hi, lo = hi_ref[at, :], lo_ref[at, :]
        right = dot(hi, h_hi) + (dot(lo, h_hi) + dot(hi, h_lo))
        for r in range(16):
            r_ref[(c + r) * GAP:(c + r) * GAP + CELLS, :] = right[r * CELLS:(r + 1) * CELLS]
    for c in range(0, CELLS, 2):
        pair = jnp.concatenate([r_ref[pl.ds(c + n, B, stride=GAP), :] for n in range(2)], axis=1)
        hi, lo = split2(pair)
        out = dot(t_hi, hi) + (dot(t_hi, lo) + dot(t_lo, hi))
        for n in range(2):
            o_ref[pl.ds(c + n, B, stride=GAP), :] = out[:, L * n:L * (n + 1)]
    for j in range(B // 4):
        for half in range(RC):
            rows = [o_ref[(4 * j + v) * GAP + 8 * half:(4 * j + v) * GAP + 8 * half + 8, :] for v in range(4)]
            for u, piece in enumerate(pack_rows(*rows)):
                last_ref[half, :, 384 * j + L * u:384 * j + L * (u + 1)] = piece


def close(received, h, ht):
    out = jax.ShapeDtypeStruct((RC, SC, WIDTH), jnp.float32)
    return pl.pallas_call(
        close_kernel,
        out_shape=(out, out),
        scratch_shapes=[
            pltpu.VMEM((4, B * 8 + 16, L), jnp.float32),
            pltpu.VMEM((B * CELLS, L), jnp.bfloat16),
            pltpu.VMEM((B * CELLS, L), jnp.bfloat16),
            pltpu.VMEM((B * GAP, L), jnp.float32),
            pltpu.VMEM((B * GAP, L), jnp.float32),
        ],
        compiler_params=pltpu.CompilerParams(vmem_limit_bytes=16 << 20),
        name="close",
    )(received, h, ht)


def local(a_blocks, a_cols, q_blocks, part_of, part_dest, part_pos, g_level):
    me = lax.axis_index("gy").astype(jnp.int32).reshape(1)
    g = g_level.reshape(3, B, B)
    mm = functools.partial(jnp.dot, precision=lax.Precision.HIGHEST)
    h = mm(mm(g[0], g[1]), g[2])
    slices = fine(a_blocks, a_cols, q_blocks, part_of, part_dest, part_pos, me)
    gathered = lax.all_to_all(slices, "gy", split_axis=0, concat_axis=0, tiled=True)
    mine, group = cells_of(gathered)
    others = [lax.ppermute(group, "gx", [(i, (i + d) % GX) for i in range(GX)]) for d in range(1, GX)]
    outgoing = merge(mine, [group] + others)
    back = lax.all_to_all(outgoing, "gy", split_axis=0, concat_axis=0, tiled=True)
    return close(back, jnp.pad(h, ((0, L - B), (0, L - B))), h.T)


def solution(mesh):
    placed = (
        P(("gx", "gy"), None, None),
        P(("gx", "gy"), None),
        P(("gx", "gy"), None),
        P(("gx", "gy"), None),
        P(("gx", "gy"), None),
        P(("gx", "gy")),
        P(),
    )
    return jax.shard_map(
        local,
        mesh=mesh,
        in_specs=placed,
        out_specs=(P(("gx", "gy"), None, None), P(("gx", "gy"), None, None)),
        check_vma=False,
    )
```

```python
import functools
import jax
import jax.numpy as jnp
from jax import lax
from jax.experimental import pallas as pl
from jax.experimental.pallas import tpu as pltpu
from jax.sharding import PartitionSpec as P

B = 96
L = 128
R = 64
KA = 8
RC = 2
SC = 8
NP = 64
CELLS = RC * SC
WIDTH = B * B
GY = 32
GX = 4
PER = B // GY
TILES = 18
ROWS_STEP = 16
STRIDE = 100
GAP = 20
M_ROWS = 512
APART = 104


def lane_iota(rows):
    return lax.broadcasted_iota(jnp.int32, (rows, L), 1)


def unpack_rows(t0, t1, t2):
    lane = lane_iota(t0.shape[0])
    r1 = jnp.where(lane < 32, pltpu.roll(t0, 32, 1), pltpu.roll(t1, 32, 1))
    r2 = jnp.where(lane < 64, pltpu.roll(t1, 64, 1), pltpu.roll(t2, 64, 1))
    return t0, r1, r2, pltpu.roll(t2, 96, 1)


def pack_rows(v0, v1, v2, v3):
    lane = lane_iota(v0.shape[0])
    s1 = pltpu.roll(v1, 96, 1)
    s2 = pltpu.roll(v2, 64, 1)
    s3 = pltpu.roll(v3, 32, 1)
    return jnp.where(lane < 96, v0, s1), jnp.where(lane < 64, s1, s2), jnp.where(lane < 32, s2, s3)


def fine_kernel(cols, part, dest, pos, me, a_ref, q_ref, x_ref, s_ref, q_mat, q_tr, acc, aq_ref):
    step = pl.program_id(0)

    def relayout(load, slot, triples):
        for j in triples:
            rows = unpack_rows(*[load(slice(384 * j + L * u, 384 * j + L * (u + 1))).astype(jnp.float32) for u in range(3)])
            for v in range(4):
                s_ref[slot, pl.ds(4 * j + v, 8, stride=STRIDE), :] = rows[v]

    @pl.when(step == 0)
    def _():
        low = lane_iota(B) < B
        unit = (lane_iota(B) == lax.broadcasted_iota(jnp.int32, (B, L), 0)).astype(jnp.bfloat16)
        part_rows = NP * APART // R

        def spread(g, triples):
            both = slice(16 * (g // 2), 16 * (g // 2) + 16)
            relayout(lambda lanes: q_ref[both, lanes][8 * (g % 2):8 * (g % 2) + 8], g % 2, triples)

        s_ref[1] = jnp.zeros((KA * STRIDE, L), jnp.float32)
        aq_ref[...] = jnp.zeros_like(aq_ref)
        spread(0, range(B // 4))
        for c in range(R):
            g, k = divmod(c, 8)
            if c + 8 < R:
                spread(g + 1, range(3 * k, 3 * k + 3))
            acc[c * part_rows:(c + 1) * part_rows, :] = jnp.zeros((part_rows, L), jnp.float32)
            mat = jnp.where(low, s_ref[g % 2, k * STRIDE:k * STRIDE + B, :], 0.0).astype(jnp.bfloat16)
            q_mat[c] = mat
            turned = lax.dot_general(unit, mat, (((1,), (1,)), ((), ())), preferred_element_type=jnp.float32)
            q_tr[c] = turned.astype(jnp.bfloat16)

    def first(r, slot, k):
        row = jnp.maximum(r, 0)
        for kk in (k, k + 1):
            mat = s_ref[slot, kk * STRIDE:kk * STRIDE + B, :].astype(jnp.bfloat16)
            prod = jnp.dot(mat[:, :B], q_mat[cols[kk, row]], preferred_element_type=jnp.float32)
            aq_ref[slot, k // 2, :, L * (kk - k):L * (kk - k + 1)] = prod.astype(jnp.bfloat16)

    def second(r, slot, k):
        row = jnp.maximum(r, 0)
        term = jnp.dot(q_tr[row], aq_ref[slot, k // 2], preferred_element_type=jnp.float32)
        for m in range(2):
            p = jnp.where(r < 0, NP, part[k + m, row])
            at = pl.ds(pl.multiple_of(p * APART, 8), B)
            acc[at, :] = acc[at, :] + term[:, L * m:L * (m + 1)]

    last = pl.num_programs(0) - 1

    @pl.when(step < last)
    def _():
        for ii in range(ROWS_STEP):
            r = step * ROWS_STEP + ii
            for n in range(4):
                first(r - 1, (ii + 1) % 2, 2 * n)
                relayout(lambda lanes: a_ref[ii, :, lanes], ii % 2, range(6 * n, 6 * n + 6))
                second(r - 2, ii % 2, 2 * n)

    @pl.when(step == last)
    def _():
        for n in range(4):
            first(R - 1, (R - 1) % 2, 2 * n)
            second(R - 2, R % 2, 2 * n)
        for n in range(4):
            second(R - 1, (R - 1) % 2, 2 * n)

    @pl.when(step == last)
    def _():
        row = lax.broadcasted_iota(jnp.int32, (8, L), 0)
        lane = lane_iota(8)
        base = (me[0] % 8) * 16
        codes = jnp.zeros((8, L), jnp.float32)
        for p in range(NP):
            codes = jnp.where((row == p // 16) & (lane == base + p % 16), (dest[p] * CELLS + pos[p]).astype(jnp.float32), codes)

        def one(w, carry):
            for a in range(PER):
                rows = [acc[pl.ds(v * 16 * APART + w * PER + a, 16, stride=APART), :] for v in range(4)]
                for u, piece in enumerate(pack_rows(*rows)):
                    for h in range(2):
                        x_ref[w, (2 * a + h) * 3 + u] = piece[8 * h:8 * h + 8]
            x_ref[w, TILES] = codes
            return carry

        lax.fori_loop(0, GY, one, 0, unroll=8)


def fine(a_blocks, a_cols, q_blocks, part_of, part_dest, part_pos, me):
    return pl.pallas_call(
        fine_kernel,
        out_shape=jax.ShapeDtypeStruct((GY, TILES + 1, 8, L), jnp.float32),
        grid_spec=pltpu.PrefetchScalarGridSpec(
            num_scalar_prefetch=5,
            grid=(R // ROWS_STEP + 1,),
            in_specs=[
                pl.BlockSpec((ROWS_STEP, KA, WIDTH), lambda g, *_: (jnp.minimum(g, R // ROWS_STEP - 1), 0, 0)),
                pl.BlockSpec((R, WIDTH), lambda g, *_: (0, 0)),
            ],
            out_specs=pl.BlockSpec((GY, TILES + 1, 8, L), lambda g, *_: (0, 0, 0, 0)),
            scratch_shapes=[
                pltpu.VMEM((2, KA * STRIDE, L), jnp.float32),
                pltpu.VMEM((R, B, L), jnp.bfloat16),
                pltpu.VMEM((R, B, B), jnp.bfloat16),
                pltpu.VMEM(((NP + 1) * APART, L), jnp.float32),
                pltpu.VMEM((2, KA // 2, B, 2 * L), jnp.bfloat16),
            ],
        ),
        compiler_params=pltpu.CompilerParams(vmem_limit_bytes=58 << 20),
        name="fine",
    )(a_cols.T, part_of.T, part_dest.reshape(NP), part_pos, me, a_blocks, q_blocks)


def split2(x):
    hi = x.astype(jnp.bfloat16)
    return hi, (x - hi.astype(jnp.float32)).astype(jnp.bfloat16)


def cells_kernel(y_ref, z_ref, t_ref, x_ref, m_ref, g_ref):
    wide = 2 * PER * L

    def one(s, carry):
        for a in range(PER):
            halves = [unpack_rows(*[y_ref[s, (2 * a + h) * 3 + u] for u in range(3)]) for h in range(2)]
            for v in range(4):
                hi, lo = split2(jnp.concatenate([halves[0][v], halves[1][v]], axis=0))
                at = pl.ds(pl.multiple_of(v * 512 + s * 16, 16), 16)
                x_ref[at, L * a:L * (a + 1)] = hi
                x_ref[at, L * (PER + a):L * (PER + a + 1)] = lo
        return carry

    lax.fori_loop(0, GY, one, 0, unroll=4)
    tiles = [functools.reduce(jnp.add, [y_ref[8 * o + s, TILES] for s in range(8)]) for o in range(4)]
    codes = jnp.concatenate([tiles[o][v:v + 1] for v in range(4) for o in range(4)], axis=1) - 256.0
    names = codes.astype(jnp.bfloat16)
    row = lax.broadcasted_iota(jnp.int32, (4 * L, 1), 0)
    want = ((row % L) // 4) * CELLS + 4 * (row // L) + row % 4
    want = (want.astype(jnp.float32) - 256.0).astype(jnp.bfloat16)
    one_bf, zero_bf = jnp.ones((), jnp.bfloat16), jnp.zeros((), jnp.bfloat16)
    for c in range(0, 4 * L, M_ROWS):
        table = jnp.where(want[c:c + M_ROWS] == names, one_bf, zero_bf)
        sums = jnp.dot(table, x_ref[...], preferred_element_type=jnp.float32)
        m_ref[c:c + M_ROWS, :] = sums[:, :wide // 2] + sums[:, wide // 2:]

    def fold(g, carry):
        for a in range(PER):
            for v in range(4):
                at = pl.multiple_of(L * v + 16 * g, 16)
                both = m_ref[pl.ds(at, 8), L * a:L * (a + 1)] + m_ref[pl.ds(at + 8, 8), L * a:L * (a + 1)]
                both = both + pltpu.roll(both, 4, 0)
                g_ref[a, v, pl.ds(pl.multiple_of(4 * g, 4), 4), :] = both[0:4]
        return carry

    lax.fori_loop(0, GY // 4, fold, 0, unroll=2)
    for a in range(PER):
        for u, piece in enumerate(pack_rows(*[g_ref[a, v] for v in range(4)])):
            t_ref[3 * a + u] = piece

    def pack(n, carry):
        for a in range(PER):
            rows = [m_ref[pl.ds(pl.multiple_of(L * v + 16 * n, 16), 16), L * a:L * (a + 1)] for v in range(4)]
            for u, piece in enumerate(pack_rows(*rows)):
                z_ref[3 * a + u, pl.ds(pl.multiple_of(16 * n, 16), 16), :] = piece
        return carry

    lax.fori_loop(0, L // 16, pack, 0, unroll=2)


def cells_of(received):
    return pl.pallas_call(
        cells_kernel,
        out_shape=(
            jax.ShapeDtypeStruct((3 * PER, L + 8, L), jnp.float32),
            jax.ShapeDtypeStruct((3 * PER, L // 4, L), jnp.float32),
        ),
        scratch_shapes=[
            pltpu.VMEM((4 * 512, 2 * PER * L), jnp.bfloat16),
            pltpu.VMEM((4 * L, PER * L), jnp.float32),
            pltpu.VMEM((PER, 4, L // 4, L), jnp.float32),
        ],
        compiler_params=pltpu.CompilerParams(vmem_limit_bytes=24 << 20),
        name="cells",
    )(received)


def merge_kernel(z_ref, t0, t1, t2, t3, out_ref, s_ref):
    upper = lax.broadcasted_iota(jnp.int32, (8, L), 0) < 4
    for n in range(3 * PER):
        s_ref[n, 4:L // 4 + 4, :] = (t0[n] + t1[n]) + (t2[n] + t3[n])
    for d in range(GY):
        g = d // 4
        for n in range(3 * PER):
            out_ref[d, n] = jnp.where(upper, z_ref[n, 4 * d:4 * d + 8, :], s_ref[n, 4 * g:4 * g + 8, :])


def merge(mine, parts):
    return pl.pallas_call(
        merge_kernel,
        out_shape=jax.ShapeDtypeStruct((GY, 3 * PER, 8, L), jnp.float32),
        scratch_shapes=[pltpu.VMEM((3 * PER, L // 4 + 8, L), jnp.float32)],
        compiler_params=pltpu.CompilerParams(vmem_limit_bytes=8 << 20),
        name="merge",
    )(mine, *parts)


def close_kernel(w_ref, h_ref, ht_ref, first_ref, last_ref, f_ref, hi_ref, lo_ref, r_ref, o_ref):
    upper = lax.broadcasted_iota(jnp.int32, (8, L), 0) < 4

    def spread(w, carry):
        for a in range(PER):
            rows = unpack_rows(*[w_ref[w, 3 * a + u] for u in range(3)])
            for v in range(4):
                f_ref[v, pl.ds(pl.multiple_of((w * PER + a) * 8 + 8, 8), 8), :] = rows[v]
        return carry

    lax.fori_loop(0, GY, spread, 0, unroll=4)

    def outputs(j, carry):
        lanes = [pl.ds(pl.multiple_of(384 * j + L * u, L), L) for u in range(3)]
        base = pl.multiple_of(32 * j + 8, 8)
        for half in range(RC):
            rows = [jnp.where(upper, f_ref[2 * half, pl.ds(base + 8 * v, 8), :], f_ref[2 * half + 1, pl.ds(base + 8 * v - 4, 8), :]) for v in range(4)]
            for u, piece in enumerate(pack_rows(*rows)):
                first_ref[half, :, lanes[u]] = piece
        for v in range(4):
            both = [jnp.where(upper, f_ref[2 * half, pl.ds(base + 8 * v + 4, 8), :], f_ref[2 * half + 1, pl.ds(base + 8 * v, 8), :]) for half in range(RC)]
            hi, lo = split2(jnp.concatenate(both, axis=0))
            at = pl.ds(pl.multiple_of(64 * j + 16 * v, 16), 16)
            hi_ref[at, :] = hi
            lo_ref[at, :] = lo
        return carry

    lax.fori_loop(0, B // 4, outputs, 0, unroll=2)
    h_hi, h_lo = split2(h_ref[...])
    t_hi, t_lo = split2(ht_ref[...])
    dot = functools.partial(jnp.dot, preferred_element_type=jnp.float32)
    for c in range(0, B, 16):
        at = slice(c * CELLS, (c + 16) * CELLS)
        hi, lo = hi_ref[at, :], lo_ref[at, :]
        right = dot(hi, h_hi) + (dot(lo, h_hi) + dot(hi, h_lo))
        for r in range(16):
            r_ref[(c + r) * GAP:(c + r) * GAP + CELLS, :] = right[r * CELLS:(r + 1) * CELLS]
    for c in range(0, CELLS, 2):
        pair = jnp.concatenate([r_ref[pl.ds(c + n, B, stride=GAP), :] for n in range(2)], axis=1)
        hi, lo = split2(pair)
        out = dot(t_hi, hi) + (dot(t_hi, lo) + dot(t_lo, hi))
        for n in range(2):
            o_ref[pl.ds(c + n, B, stride=GAP), :] = out[:, L * n:L * (n + 1)]
    for j in range(B // 4):
        for half in range(RC):
            rows = [o_ref[(4 * j + v) * GAP + 8 * half:(4 * j + v) * GAP + 8 * half + 8, :] for v in range(4)]
            for u, piece in enumerate(pack_rows(*rows)):
                last_ref[half, :, 384 * j + L * u:384 * j + L * (u + 1)] = piece


def close(received, h, ht):
    out = jax.ShapeDtypeStruct((RC, SC, WIDTH), jnp.float32)
    return pl.pallas_call(
        close_kernel,
        out_shape=(out, out),
        scratch_shapes=[
            pltpu.VMEM((4, B * 8 + 16, L), jnp.float32),
            pltpu.VMEM((B * CELLS, L), jnp.bfloat16),
            pltpu.VMEM((B * CELLS, L), jnp.bfloat16),
            pltpu.VMEM((B * GAP, L), jnp.float32),
            pltpu.VMEM((B * GAP, L), jnp.float32),
        ],
        compiler_params=pltpu.CompilerParams(vmem_limit_bytes=16 << 20),
        name="close",
    )(received, h, ht)


def local(a_blocks, a_cols, q_blocks, part_of, part_dest, part_pos, g_level):
    me = lax.axis_index("gy").astype(jnp.int32).reshape(1)
    g = g_level.reshape(3, B, B)
    mm = functools.partial(jnp.dot, precision=lax.Precision.HIGHEST)
    h = mm(mm(g[0], g[1]), g[2])
    slices = fine(a_blocks, a_cols, q_blocks, part_of, part_dest, part_pos, me)
    gathered = lax.all_to_all(slices, "gy", split_axis=0, concat_axis=0, tiled=True)
    mine, group = cells_of(gathered)
    others = [lax.ppermute(group, "gx", [(i, (i + d) % GX) for i in range(GX)]) for d in range(1, GX)]
    outgoing = merge(mine, [group] + others)
    back = lax.all_to_all(outgoing, "gy", split_axis=0, concat_axis=0, tiled=True)
    return close(back, jnp.pad(h, ((0, L - B), (0, L - B))), h.T)


def solution(mesh):
    placed = (
        P(("gx", "gy"), None, None),
        P(("gx", "gy"), None),
        P(("gx", "gy"), None),
        P(("gx", "gy"), None),
        P(("gx", "gy"), None),
        P(("gx", "gy")),
        P(),
    )
    return jax.shard_map(
        local,
        mesh=mesh,
        in_specs=placed,
        out_specs=(P(("gx", "gy"), None, None), P(("gx", "gy"), None, None)),
        check_vma=False,
    )
```

```python
import functools
import jax
import jax.numpy as jnp
from jax import lax
from jax.experimental import pallas as pl
from jax.experimental.pallas import tpu as pltpu
from jax.sharding import PartitionSpec as P

B = 96
L = 128
R = 64
KA = 8
RC = 2
SC = 8
NP = 64
CELLS = RC * SC
WIDTH = B * B
GY = 32
GX = 4
PER = B // GY
TILES = 18
ROWS_STEP = 16
STRIDE = 100
GAP = 20
M_ROWS = 512
HALF = (3 * PER + 1) // 2
APART = 104


def lane_iota(rows):
    return lax.broadcasted_iota(jnp.int32, (rows, L), 1)


def unpack_rows(t0, t1, t2):
    lane = lane_iota(t0.shape[0])
    r1 = jnp.where(lane < 32, pltpu.roll(t0, 32, 1), pltpu.roll(t1, 32, 1))
    r2 = jnp.where(lane < 64, pltpu.roll(t1, 64, 1), pltpu.roll(t2, 64, 1))
    return t0, r1, r2, pltpu.roll(t2, 96, 1)


def pack_rows(v0, v1, v2, v3):
    lane = lane_iota(v0.shape[0])
    s1 = pltpu.roll(v1, 96, 1)
    s2 = pltpu.roll(v2, 64, 1)
    s3 = pltpu.roll(v3, 32, 1)
    return jnp.where(lane < 96, v0, s1), jnp.where(lane < 64, s1, s2), jnp.where(lane < 32, s2, s3)


def fine_kernel(cols, part, dest, pos, me, a_ref, q_ref, x_ref, s_ref, q_mat, q_tr, acc, aq_ref):
    step = pl.program_id(0)

    def relayout(load, slot, triples):
        for j in triples:
            rows = unpack_rows(*[load(slice(384 * j + L * u, 384 * j + L * (u + 1))).astype(jnp.float32) for u in range(3)])
            for v in range(4):
                s_ref[slot, pl.ds(4 * j + v, 8, stride=STRIDE), :] = rows[v]

    @pl.when(step == 0)
    def _():
        low = lane_iota(B) < B
        unit = (lane_iota(B) == lax.broadcasted_iota(jnp.int32, (B, L), 0)).astype(jnp.bfloat16)
        part_rows = NP * APART // R

        def spread(g, triples):
            both = slice(16 * (g // 2), 16 * (g // 2) + 16)
            relayout(lambda lanes: q_ref[both, lanes][8 * (g % 2):8 * (g % 2) + 8], g % 2, triples)

        s_ref[1] = jnp.zeros((KA * STRIDE, L), jnp.float32)
        aq_ref[...] = jnp.zeros_like(aq_ref)
        spread(0, range(B // 4))
        for c in range(R):
            g, k = divmod(c, 8)
            if c + 8 < R:
                spread(g + 1, range(3 * k, 3 * k + 3))
            acc[c * part_rows:(c + 1) * part_rows, :] = jnp.zeros((part_rows, L), jnp.float32)
            mat = jnp.where(low, s_ref[g % 2, k * STRIDE:k * STRIDE + B, :], 0.0).astype(jnp.bfloat16)
            q_mat[c] = mat
            turned = lax.dot_general(unit, mat, (((1,), (1,)), ((), ())), preferred_element_type=jnp.float32)
            q_tr[c] = turned.astype(jnp.bfloat16)

    def first(r, slot, k):
        row = jnp.maximum(r, 0)
        for kk in (k, k + 1):
            mat = s_ref[slot, kk * STRIDE:kk * STRIDE + B, :].astype(jnp.bfloat16)
            prod = jnp.dot(mat[:, :B], q_mat[cols[kk, row]], preferred_element_type=jnp.float32)
            aq_ref[slot, k // 2, :, L * (kk - k):L * (kk - k + 1)] = prod.astype(jnp.bfloat16)

    def second(r, slot, k):
        row = jnp.maximum(r, 0)
        term = jnp.dot(q_tr[row], aq_ref[slot, k // 2], preferred_element_type=jnp.float32)
        for m in range(2):
            p = jnp.where(r < 0, NP, part[k + m, row])
            at = pl.ds(pl.multiple_of(p * APART, 8), B)
            acc[at, :] = acc[at, :] + term[:, L * m:L * (m + 1)]

    last = pl.num_programs(0) - 1

    @pl.when(step < last)
    def _():
        for ii in range(ROWS_STEP):
            r = step * ROWS_STEP + ii
            for n in range(4):
                first(r - 1, (ii + 1) % 2, 2 * n)
                relayout(lambda lanes: a_ref[ii, :, lanes], ii % 2, range(6 * n, 6 * n + 6))
                second(r - 2, ii % 2, 2 * n)

    @pl.when(step == last)
    def _():
        for n in range(4):
            first(R - 1, (R - 1) % 2, 2 * n)
            second(R - 2, R % 2, 2 * n)
        for n in range(4):
            second(R - 1, (R - 1) % 2, 2 * n)

    @pl.when(step == last)
    def _():
        row = lax.broadcasted_iota(jnp.int32, (8, L), 0)
        lane = lane_iota(8)
        base = (me[0] % 8) * 16
        codes = jnp.zeros((8, L), jnp.float32)
        for p in range(NP):
            codes = jnp.where((row == p // 16) & (lane == base + p % 16), (dest[p] * CELLS + pos[p]).astype(jnp.float32), codes)

        def one(w, carry):
            for a in range(PER):
                rows = [acc[pl.ds(v * 16 * APART + w * PER + a, 16, stride=APART), :] for v in range(4)]
                for u, piece in enumerate(pack_rows(*rows)):
                    for h in range(2):
                        x_ref[w, (2 * a + h) * 3 + u] = piece[8 * h:8 * h + 8]
            x_ref[w, TILES] = codes
            return carry

        lax.fori_loop(0, GY, one, 0, unroll=8)


def fine(a_blocks, a_cols, q_blocks, part_of, part_dest, part_pos, me):
    return pl.pallas_call(
        fine_kernel,
        out_shape=jax.ShapeDtypeStruct((GY, TILES + 1, 8, L), jnp.float32),
        grid_spec=pltpu.PrefetchScalarGridSpec(
            num_scalar_prefetch=5,
            grid=(R // ROWS_STEP + 1,),
            in_specs=[
                pl.BlockSpec((ROWS_STEP, KA, WIDTH), lambda g, *_: (jnp.minimum(g, R // ROWS_STEP - 1), 0, 0)),
                pl.BlockSpec((R, WIDTH), lambda g, *_: (0, 0)),
            ],
            out_specs=pl.BlockSpec((GY, TILES + 1, 8, L), lambda g, *_: (0, 0, 0, 0)),
            scratch_shapes=[
                pltpu.VMEM((2, KA * STRIDE, L), jnp.float32),
                pltpu.VMEM((R, B, L), jnp.bfloat16),
                pltpu.VMEM((R, B, B), jnp.bfloat16),
                pltpu.VMEM(((NP + 1) * APART, L), jnp.float32),
                pltpu.VMEM((2, KA // 2, B, 2 * L), jnp.bfloat16),
            ],
        ),
        compiler_params=pltpu.CompilerParams(vmem_limit_bytes=58 << 20),
        name="fine",
    )(a_cols.T, part_of.T, part_dest.reshape(NP), part_pos, me, a_blocks, q_blocks)


def split2(x):
    hi = x.astype(jnp.bfloat16)
    return hi, (x - hi.astype(jnp.float32)).astype(jnp.bfloat16)


def cells_kernel(y_ref, z_ref, t_ref, x_ref, m_ref, g_ref, p_ref):
    wide = 2 * PER * L

    def one(s, carry):
        for a in range(PER):
            halves = [unpack_rows(*[y_ref[s, (2 * a + h) * 3 + u] for u in range(3)]) for h in range(2)]
            for v in range(4):
                hi, lo = split2(jnp.concatenate([halves[0][v], halves[1][v]], axis=0))
                at = pl.ds(pl.multiple_of(v * 512 + s * 16, 16), 16)
                x_ref[at, L * a:L * (a + 1)] = hi
                x_ref[at, L * (PER + a):L * (PER + a + 1)] = lo
        return carry

    lax.fori_loop(0, GY, one, 0, unroll=4)
    tiles = [functools.reduce(jnp.add, [y_ref[8 * o + s, TILES] for s in range(8)]) for o in range(4)]
    codes = jnp.concatenate([tiles[o][v:v + 1] for v in range(4) for o in range(4)], axis=1) - 256.0
    names = codes.astype(jnp.bfloat16)
    row = lax.broadcasted_iota(jnp.int32, (4 * L, 1), 0)
    want = ((row % L) // 4) * CELLS + 4 * (row // L) + row % 4
    want = (want.astype(jnp.float32) - 256.0).astype(jnp.bfloat16)
    one_bf, zero_bf = jnp.ones((), jnp.bfloat16), jnp.zeros((), jnp.bfloat16)
    for c in range(0, 4 * L, M_ROWS):
        table = jnp.where(want[c:c + M_ROWS] == names, one_bf, zero_bf)
        sums = jnp.dot(table, x_ref[...], preferred_element_type=jnp.float32)
        m_ref[c:c + M_ROWS, :] = sums[:, :wide // 2] + sums[:, wide // 2:]

    def fold(g, carry):
        for a in range(PER):
            for v in range(4):
                at = pl.multiple_of(L * v + 16 * g, 16)
                both = m_ref[pl.ds(at, 8), L * a:L * (a + 1)] + m_ref[pl.ds(at + 8, 8), L * a:L * (a + 1)]
                both = both + pltpu.roll(both, 4, 0)
                g_ref[a, v, pl.ds(pl.multiple_of(4 * g, 4), 4), :] = both[0:4]
        return carry

    lax.fori_loop(0, GY // 4, fold, 0, unroll=2)
    for a in range(PER):
        for u, piece in enumerate(pack_rows(*[g_ref[a, v] for v in range(4)])):
            t_ref[3 * a + u] = piece

    def pack(n, carry):
        for a in range(PER):
            rows = [m_ref[pl.ds(pl.multiple_of(L * v + 16 * n, 16), 16), L * a:L * (a + 1)] for v in range(4)]
            for u, piece in enumerate(pack_rows(*rows)):
                p_ref[3 * a + u, pl.ds(pl.multiple_of(16 * n + 8, 8), 16), :] = piece
        return carry

    lax.fori_loop(0, L // 16, pack, 0, unroll=2)
    for d in range(GY):
        for t in range(HALF):
            z_ref[d, 8 * t:8 * t + 8, :] = two_halves(p_ref, t, 4 * d + 8)


def two_halves(ref, t, at):
    one = ref[2 * t, at:at + 8, :]
    if 2 * t + 1 == 3 * PER:
        return one
    upper = lax.broadcasted_iota(jnp.int32, (8, L), 0) < 4
    return jnp.where(upper, one, ref[2 * t + 1, at - 4:at + 4, :])


def cells_of(received):
    return pl.pallas_call(
        cells_kernel,
        out_shape=(
            jax.ShapeDtypeStruct((GY, 8 * HALF, L), jnp.float32),
            jax.ShapeDtypeStruct((3 * PER, L // 4, L), jnp.float32),
        ),
        scratch_shapes=[
            pltpu.VMEM((4 * 512, 2 * PER * L), jnp.bfloat16),
            pltpu.VMEM((4 * L, PER * L), jnp.float32),
            pltpu.VMEM((PER, 4, L // 4, L), jnp.float32),
            pltpu.VMEM((3 * PER, L + 16, L), jnp.float32),
        ],
        compiler_params=pltpu.CompilerParams(vmem_limit_bytes=24 << 20),
        name="cells",
    )(received)


def merge_kernel(t0, t1, t2, t3, out_ref, s_ref):
    for n in range(3 * PER):
        s_ref[n, 8:L // 4 + 8, :] = (t0[n] + t1[n]) + (t2[n] + t3[n])
    for g in range(GY // 4):
        for t in range(HALF):
            tile = two_halves(s_ref, t, 4 * g + 8)
            for m in range(4):
                out_ref[4 * g + m, 8 * t:8 * t + 8, :] = tile


def merge(*parts):
    return pl.pallas_call(
        merge_kernel,
        out_shape=jax.ShapeDtypeStruct((GY, 8 * HALF, L), jnp.float32),
        scratch_shapes=[pltpu.VMEM((3 * PER, L // 4 + 16, L), jnp.float32)],
        compiler_params=pltpu.CompilerParams(vmem_limit_bytes=8 << 20),
        cost_estimate=pl.CostEstimate(flops=1 << 20, bytes_accessed=2 << 20, transcendentals=0),
        name="merge",
    )(*parts)


def spread_cells(w_ref, f_ref):
    upper = lax.broadcasted_iota(jnp.int32, (8, L), 0) < 4

    def pair(n, carry):
        w = 2 * n
        for a in range(PER):
            at = []
            for u in range(3):
                k = 4 * (3 * a + u)
                other = w_ref[w + 1, k - 4:k + 4, :] if k else pltpu.roll(w_ref[w + 1, 0:8, :], 4, 0)
                at.append(jnp.where(upper, w_ref[w, k:k + 8, :], other))
            for v, rows in enumerate(unpack_rows(*at)):
                f_ref[v, a, pl.ds(pl.multiple_of(8 * n + 8, 8), 8), :] = rows
        return carry

    lax.fori_loop(0, GY // 2, pair, 0, unroll=4)


def cell_rows(f_ref, w, a, half):
    upper = lax.broadcasted_iota(jnp.int32, (8, L), 0) < 4
    return jnp.where(upper, f_ref[2 * half, a, pl.ds(4 * w + 8, 8), :], f_ref[2 * half + 1, a, pl.ds(4 * w + 4, 8), :])


def first_kernel(w_ref, first_ref, f_ref):
    spread_cells(w_ref, f_ref)

    def outputs(n, carry):
        for j in range(PER):
            lanes = [pl.ds(pl.multiple_of(384 * (PER * n + j) + L * u, L), L) for u in range(3)]
            for half in range(RC):
                rows = [cell_rows(f_ref, 4 * n + (4 * j + v) // PER, (4 * j + v) % PER, half) for v in range(4)]
                for u, piece in enumerate(pack_rows(*rows)):
                    first_ref[half, :, lanes[u]] = piece
        return carry

    lax.fori_loop(0, GY // 4, outputs, 0)


def close_kernel(w_ref, h_ref, ht_ref, last_ref, f_ref, hi_ref, lo_ref, r_ref, o_ref):
    spread_cells(w_ref, f_ref)

    def pieces(n, carry):
        for i in range(2):
            for a in range(PER):
                w = 2 * n + i
                hi, lo = split2(jnp.concatenate([cell_rows(f_ref, w, a, half) for half in range(RC)], axis=0))
                at = pl.ds(pl.multiple_of(CELLS * (PER * w + a), CELLS), CELLS)
                hi_ref[at, :] = hi
                lo_ref[at, :] = lo
        return carry

    lax.fori_loop(0, GY // 2, pieces, 0)
    h_hi, h_lo = split2(h_ref[...])
    t_hi, t_lo = split2(ht_ref[...])
    dot = functools.partial(jnp.dot, preferred_element_type=jnp.float32)
    for c in range(0, B, 16):
        at = slice(c * CELLS, (c + 16) * CELLS)
        hi, lo = hi_ref[at, :], lo_ref[at, :]
        right = dot(hi, h_hi) + (dot(lo, h_hi) + dot(hi, h_lo))
        for r in range(16):
            r_ref[(c + r) * GAP:(c + r) * GAP + CELLS, :] = right[r * CELLS:(r + 1) * CELLS]
    for c in range(0, CELLS, 2):
        pair = jnp.concatenate([r_ref[pl.ds(c + n, B, stride=GAP), :] for n in range(2)], axis=1)
        hi, lo = split2(pair)
        out = dot(t_hi, hi) + (dot(t_hi, lo) + dot(t_lo, hi))
        for n in range(2):
            o_ref[pl.ds(c + n, B, stride=GAP), :] = out[:, L * n:L * (n + 1)]
    for j in range(B // 4):
        for half in range(RC):
            rows = [o_ref[(4 * j + v) * GAP + 8 * half:(4 * j + v) * GAP + 8 * half + 8, :] for v in range(4)]
            for u, piece in enumerate(pack_rows(*rows)):
                last_ref[half, :, 384 * j + L * u:384 * j + L * (u + 1)] = piece


def finish(kernel, name, scratch, *operands):
    return pl.pallas_call(
        kernel,
        out_shape=jax.ShapeDtypeStruct((RC, SC, WIDTH), jnp.float32),
        scratch_shapes=[pltpu.VMEM((4, PER, 4 * GY + 16, L), jnp.float32)] + scratch,
        compiler_params=pltpu.CompilerParams(vmem_limit_bytes=16 << 20),
        cost_estimate=pl.CostEstimate(flops=1 << 20, bytes_accessed=4 << 20, transcendentals=0),
        name=name,
    )(*operands)


def local(a_blocks, a_cols, q_blocks, part_of, part_dest, part_pos, g_level):
    me = lax.axis_index("gy").astype(jnp.int32).reshape(1)
    g = g_level.reshape(3, B, B)
    mm = functools.partial(jnp.dot, precision=lax.Precision.HIGHEST)
    h = mm(mm(g[0], g[1]), g[2])
    slices = fine(a_blocks, a_cols, q_blocks, part_of, part_dest, part_pos, me)
    gathered = lax.all_to_all(slices, "gy", split_axis=0, concat_axis=0, tiled=True)
    mine, group = cells_of(gathered)
    others = [lax.ppermute(group, "gx", [(i, (i + d) % GX) for i in range(GX)]) for d in range(1, GX)]
    send = functools.partial(lax.all_to_all, axis_name="gy", split_axis=0, concat_axis=0, tiled=True)
    first = send(mine)
    total = send(merge(group, *others))
    coarse = finish(first_kernel, "first", [], first)
    scratch = [pltpu.VMEM((B * CELLS, L), jnp.bfloat16)] * 2 + [pltpu.VMEM((B * GAP, L), jnp.float32)] * 2
    last = finish(close_kernel, "close", scratch, total, jnp.pad(h, ((0, L - B), (0, L - B))), h.T)
    return coarse, last


def solution(mesh):
    placed = (
        P(("gx", "gy"), None, None),
        P(("gx", "gy"), None),
        P(("gx", "gy"), None),
        P(("gx", "gy"), None),
        P(("gx", "gy"), None),
        P(("gx", "gy")),
        P(),
    )
    return jax.shard_map(
        local,
        mesh=mesh,
        in_specs=placed,
        out_specs=(P(("gx", "gy"), None, None), P(("gx", "gy"), None, None)),
        check_vma=False,
    )
```

```python
import functools
import jax
import jax.numpy as jnp
from jax import lax
from jax.experimental import pallas as pl
from jax.experimental.pallas import tpu as pltpu
from jax.sharding import PartitionSpec as P

B = 96
L = 128
R = 64
KA = 8
RC = 2
SC = 8
NP = 64
CELLS = RC * SC
WIDTH = B * B
GY = 32
GX = 4
PER = B // GY
TILES = 18
ROWS_STEP = 16
STRIDE = 100
GAP = 20
M_ROWS = 512
HALF = (3 * PER + 1) // 2
APART = 104


def lane_iota(rows):
    return lax.broadcasted_iota(jnp.int32, (rows, L), 1)


def unpack_rows(t0, t1, t2):
    lane = lane_iota(t0.shape[0])
    r1 = jnp.where(lane < 32, pltpu.roll(t0, 32, 1), pltpu.roll(t1, 32, 1))
    r2 = jnp.where(lane < 64, pltpu.roll(t1, 64, 1), pltpu.roll(t2, 64, 1))
    return t0, r1, r2, pltpu.roll(t2, 96, 1)


def pack_rows(v0, v1, v2, v3):
    lane = lane_iota(v0.shape[0])
    s1 = pltpu.roll(v1, 96, 1)
    s2 = pltpu.roll(v2, 64, 1)
    s3 = pltpu.roll(v3, 32, 1)
    return jnp.where(lane < 96, v0, s1), jnp.where(lane < 64, s1, s2), jnp.where(lane < 32, s2, s3)


def fine_kernel(cols, part, dest, pos, me, a_ref, q_ref, x_ref, s_ref, q_mat, q_tr, acc, aq_ref):
    step = pl.program_id(0)

    def relayout(load, slot, triples):
        for j in triples:
            rows = unpack_rows(*[load(slice(384 * j + L * u, 384 * j + L * (u + 1))).astype(jnp.float32) for u in range(3)])
            for v in range(4):
                s_ref[slot, pl.ds(4 * j + v, 8, stride=STRIDE), :] = rows[v]

    @pl.when(step == 0)
    def _():
        low = lane_iota(B) < B
        unit = (lane_iota(B) == lax.broadcasted_iota(jnp.int32, (B, L), 0)).astype(jnp.bfloat16)
        part_rows = NP * APART // R

        def spread(g, triples):
            both = slice(16 * (g // 2), 16 * (g // 2) + 16)
            relayout(lambda lanes: q_ref[both, lanes][8 * (g % 2):8 * (g % 2) + 8], g % 2, triples)

        s_ref[1] = jnp.zeros((KA * STRIDE, L), jnp.float32)
        aq_ref[...] = jnp.zeros_like(aq_ref)
        spread(0, range(B // 4))
        for c in range(R):
            g, k = divmod(c, 8)
            if c + 8 < R:
                spread(g + 1, range(3 * k, 3 * k + 3))
            acc[c * part_rows:(c + 1) * part_rows, :] = jnp.zeros((part_rows, L), jnp.float32)
            mat = jnp.where(low, s_ref[g % 2, k * STRIDE:k * STRIDE + B, :], 0.0).astype(jnp.bfloat16)
            q_mat[c] = mat
            turned = lax.dot_general(unit, mat, (((1,), (1,)), ((), ())), preferred_element_type=jnp.float32)
            q_tr[c] = turned.astype(jnp.bfloat16)

    def first(r, slot, k):
        row = jnp.maximum(r, 0)
        for kk in (k, k + 1):
            mat = s_ref[slot, kk * STRIDE:kk * STRIDE + B, :].astype(jnp.bfloat16)
            prod = jnp.dot(mat[:, :B], q_mat[cols[kk, row]], preferred_element_type=jnp.float32)
            aq_ref[slot, k // 2, :, L * (kk - k):L * (kk - k + 1)] = prod.astype(jnp.bfloat16)

    def second(r, slot, k):
        row = jnp.maximum(r, 0)
        term = jnp.dot(q_tr[row], aq_ref[slot, k // 2], preferred_element_type=jnp.float32)
        for m in range(2):
            p = jnp.where(r < 0, NP, part[k + m, row])
            at = pl.ds(pl.multiple_of(p * APART, 8), B)
            acc[at, :] = acc[at, :] + term[:, L * m:L * (m + 1)]

    last = pl.num_programs(0) - 1

    @pl.when(step < last)
    def _():
        for ii in range(ROWS_STEP):
            r = step * ROWS_STEP + ii
            for n in range(4):
                first(r - 1, (ii + 1) % 2, 2 * n)
                relayout(lambda lanes: a_ref[ii, :, lanes], ii % 2, range(6 * n, 6 * n + 6))
                second(r - 2, ii % 2, 2 * n)

    @pl.when(step == last)
    def _():
        for n in range(4):
            first(R - 1, (R - 1) % 2, 2 * n)
            second(R - 2, R % 2, 2 * n)
        for n in range(4):
            second(R - 1, (R - 1) % 2, 2 * n)

    @pl.when(step == last)
    def _():
        row = lax.broadcasted_iota(jnp.int32, (8, L), 0)
        lane = lane_iota(8)
        base = (me[0] % 8) * 16
        codes = jnp.zeros((8, L), jnp.float32)
        for p in range(NP):
            codes = jnp.where((row == p // 16) & (lane == base + p % 16), (dest[p] * CELLS + pos[p]).astype(jnp.float32), codes)

        def one(w, carry):
            for a in range(PER):
                rows = [acc[pl.ds(v * 16 * APART + w * PER + a, 16, stride=APART), :] for v in range(4)]
                for u, piece in enumerate(pack_rows(*rows)):
                    for h in range(2):
                        x_ref[w, (2 * a + h) * 3 + u] = piece[8 * h:8 * h + 8]
            x_ref[w, TILES] = codes
            return carry

        lax.fori_loop(0, GY, one, 0, unroll=8)


def fine(a_blocks, a_cols, q_blocks, part_of, part_dest, part_pos, me):
    return pl.pallas_call(
        fine_kernel,
        out_shape=jax.ShapeDtypeStruct((GY, TILES + 1, 8, L), jnp.float32),
        grid_spec=pltpu.PrefetchScalarGridSpec(
            num_scalar_prefetch=5,
            grid=(R // ROWS_STEP + 1,),
            in_specs=[
                pl.BlockSpec((ROWS_STEP, KA, WIDTH), lambda g, *_: (jnp.minimum(g, R // ROWS_STEP - 1), 0, 0)),
                pl.BlockSpec((R, WIDTH), lambda g, *_: (0, 0)),
            ],
            out_specs=pl.BlockSpec((GY, TILES + 1, 8, L), lambda g, *_: (0, 0, 0, 0)),
            scratch_shapes=[
                pltpu.VMEM((2, KA * STRIDE, L), jnp.float32),
                pltpu.VMEM((R, B, L), jnp.bfloat16),
                pltpu.VMEM((R, B, B), jnp.bfloat16),
                pltpu.VMEM(((NP + 1) * APART, L), jnp.float32),
                pltpu.VMEM((2, KA // 2, B, 2 * L), jnp.bfloat16),
            ],
        ),
        compiler_params=pltpu.CompilerParams(vmem_limit_bytes=58 << 20),
        name="fine",
    )(a_cols.T, part_of.T, part_dest.reshape(NP), part_pos, me, a_blocks, q_blocks)


def split2(x):
    hi = x.astype(jnp.bfloat16)
    return hi, (x - hi.astype(jnp.float32)).astype(jnp.bfloat16)


def cells_kernel(y_ref, z_ref, t_ref, x_ref, m_ref, g_ref, p_ref):
    wide = 2 * PER * L

    def one(s, carry):
        for a in range(PER):
            halves = [unpack_rows(*[y_ref[s, (2 * a + h) * 3 + u] for u in range(3)]) for h in range(2)]
            for v in range(4):
                hi, lo = split2(jnp.concatenate([halves[0][v], halves[1][v]], axis=0))
                at = pl.ds(pl.multiple_of(v * 512 + s * 16, 16), 16)
                x_ref[at, L * a:L * (a + 1)] = hi
                x_ref[at, L * (PER + a):L * (PER + a + 1)] = lo
        return carry

    lax.fori_loop(0, GY, one, 0, unroll=4)
    tiles = [functools.reduce(jnp.add, [y_ref[8 * o + s, TILES] for s in range(8)]) for o in range(4)]
    codes = jnp.concatenate([tiles[o][v:v + 1] for v in range(4) for o in range(4)], axis=1) - 256.0
    names = codes.astype(jnp.bfloat16)
    row = lax.broadcasted_iota(jnp.int32, (4 * L, 1), 0)
    want = ((row % L) // 4) * CELLS + 4 * (row // L) + row % 4
    want = (want.astype(jnp.float32) - 256.0).astype(jnp.bfloat16)
    one_bf, zero_bf = jnp.ones((), jnp.bfloat16), jnp.zeros((), jnp.bfloat16)
    for c in range(0, 4 * L, M_ROWS):
        table = jnp.where(want[c:c + M_ROWS] == names, one_bf, zero_bf)
        sums = jnp.dot(table, x_ref[...], preferred_element_type=jnp.float32)
        m_ref[c:c + M_ROWS, :] = sums[:, :wide // 2] + sums[:, wide // 2:]

    def fold(g, carry):
        for a in range(PER):
            for v in range(4):
                at = pl.multiple_of(L * v + 16 * g, 16)
                both = m_ref[pl.ds(at, 8), L * a:L * (a + 1)] + m_ref[pl.ds(at + 8, 8), L * a:L * (a + 1)]
                both = both + pltpu.roll(both, 4, 0)
                g_ref[a, v, pl.ds(pl.multiple_of(4 * g, 4), 4), :] = both[0:4]
        return carry

    lax.fori_loop(0, GY // 4, fold, 0, unroll=2)
    for a in range(PER):
        for u, piece in enumerate(pack_rows(*[g_ref[a, v] for v in range(4)])):
            t_ref[3 * a + u] = piece

    def pack(n, carry):
        for a in range(PER):
            rows = [m_ref[pl.ds(pl.multiple_of(L * v + 16 * n, 16), 16), L * a:L * (a + 1)] for v in range(4)]
            for u, piece in enumerate(pack_rows(*rows)):
                p_ref[3 * a + u, pl.ds(pl.multiple_of(16 * n + 8, 8), 16), :] = piece
        return carry

    lax.fori_loop(0, L // 16, pack, 0, unroll=2)
    for d in range(GY):
        for t in range(HALF):
            z_ref[d, 8 * t:8 * t + 8, :] = two_halves(p_ref, t, 4 * d + 8)


def two_halves(ref, t, at):
    one = ref[2 * t, at:at + 8, :]
    if 2 * t + 1 == 3 * PER:
        return one
    upper = lax.broadcasted_iota(jnp.int32, (8, L), 0) < 4
    return jnp.where(upper, one, ref[2 * t + 1, at - 4:at + 4, :])


def cells_of(received):
    return pl.pallas_call(
        cells_kernel,
        out_shape=(
            jax.ShapeDtypeStruct((GY, 8 * HALF, L), jnp.float32),
            jax.ShapeDtypeStruct((3 * PER, L // 4, L), jnp.float32),
        ),
        scratch_shapes=[
            pltpu.VMEM((4 * 512, 2 * PER * L), jnp.bfloat16),
            pltpu.VMEM((4 * L, PER * L), jnp.float32),
            pltpu.VMEM((PER, 4, L // 4, L), jnp.float32),
            pltpu.VMEM((3 * PER, L + 16, L), jnp.float32),
        ],
        compiler_params=pltpu.CompilerParams(vmem_limit_bytes=24 << 20),
        name="cells",
    )(received)


def merge_kernel(t0, t1, t2, t3, out_ref, s_ref):
    for n in range(3 * PER):
        s_ref[n, 8:L // 4 + 8, :] = (t0[n] + t1[n]) + (t2[n] + t3[n])
    for g in range(GY // 4):
        for t in range(HALF):
            tile = two_halves(s_ref, t, 4 * g + 8)
            for m in range(4):
                out_ref[4 * g + m, 8 * t:8 * t + 8, :] = tile


def merge(*parts):
    return pl.pallas_call(
        merge_kernel,
        out_shape=jax.ShapeDtypeStruct((GY, 8 * HALF, L), jnp.float32),
        scratch_shapes=[pltpu.VMEM((3 * PER, L // 4 + 16, L), jnp.float32)],
        compiler_params=pltpu.CompilerParams(vmem_limit_bytes=8 << 20),
        cost_estimate=pl.CostEstimate(flops=1 << 20, bytes_accessed=2 << 20, transcendentals=0),
        name="merge",
    )(*parts)


def spread_cells(w_ref, f_ref):
    upper = lax.broadcasted_iota(jnp.int32, (8, L), 0) < 4

    def pair(n, carry):
        w = 2 * n
        for a in range(PER):
            at = []
            for u in range(3):
                k = 4 * (3 * a + u)
                other = w_ref[w + 1, k - 4:k + 4, :] if k else pltpu.roll(w_ref[w + 1, 0:8, :], 4, 0)
                at.append(jnp.where(upper, w_ref[w, k:k + 8, :], other))
            for v, rows in enumerate(unpack_rows(*at)):
                f_ref[v, a, pl.ds(pl.multiple_of(8 * n + 8, 8), 8), :] = rows
        return carry

    lax.fori_loop(0, GY // 2, pair, 0, unroll=4)


def cell_rows(f_ref, w, a, half):
    upper = lax.broadcasted_iota(jnp.int32, (8, L), 0) < 4
    return jnp.where(upper, f_ref[2 * half, a, pl.ds(4 * w + 8, 8), :], f_ref[2 * half + 1, a, pl.ds(4 * w + 4, 8), :])


def first_kernel(w_ref, first_ref, f_ref):
    spread_cells(w_ref, f_ref)

    def outputs(n, carry):
        for j in range(PER):
            lanes = [pl.ds(pl.multiple_of(384 * (PER * n + j) + L * u, L), L) for u in range(3)]
            for half in range(RC):
                rows = [cell_rows(f_ref, 4 * n + (4 * j + v) // PER, (4 * j + v) % PER, half) for v in range(4)]
                for u, piece in enumerate(pack_rows(*rows)):
                    first_ref[half, :, lanes[u]] = piece
        return carry

    lax.fori_loop(0, GY // 4, outputs, 0)


def close_kernel(w_ref, h_ref, ht_ref, last_ref, f_ref, hi_ref, lo_ref, r_ref, o_ref):
    spread_cells(w_ref, f_ref)

    def pieces(n, carry):
        for i in range(2):
            for a in range(PER):
                w = 2 * n + i
                hi, lo = split2(jnp.concatenate([cell_rows(f_ref, w, a, half) for half in range(RC)], axis=0))
                at = pl.ds(pl.multiple_of(CELLS * (PER * w + a), CELLS), CELLS)
                hi_ref[at, :] = hi
                lo_ref[at, :] = lo
        return carry

    lax.fori_loop(0, GY // 2, pieces, 0)
    h_hi, h_lo = split2(h_ref[...])
    t_hi, t_lo = split2(ht_ref[...])
    dot = functools.partial(jnp.dot, preferred_element_type=jnp.float32)
    for c in range(0, B, 16):
        at = slice(c * CELLS, (c + 16) * CELLS)
        hi, lo = hi_ref[at, :], lo_ref[at, :]
        right = dot(hi, h_hi) + (dot(lo, h_hi) + dot(hi, h_lo))
        for r in range(16):
            r_ref[(c + r) * GAP:(c + r) * GAP + CELLS, :] = right[r * CELLS:(r + 1) * CELLS]
    for c in range(0, CELLS, 2):
        pair = jnp.concatenate([r_ref[pl.ds(c + n, B, stride=GAP), :] for n in range(2)], axis=1)
        hi, lo = split2(pair)
        out = dot(t_hi, hi) + (dot(t_hi, lo) + dot(t_lo, hi))
        for n in range(2):
            o_ref[pl.ds(c + n, B, stride=GAP), :] = out[:, L * n:L * (n + 1)]
    for j in range(B // 4):
        for half in range(RC):
            rows = [o_ref[(4 * j + v) * GAP + 8 * half:(4 * j + v) * GAP + 8 * half + 8, :] for v in range(4)]
            for u, piece in enumerate(pack_rows(*rows)):
                last_ref[half, :, 384 * j + L * u:384 * j + L * (u + 1)] = piece


def finish(kernel, scratch, *operands):
    return pl.pallas_call(
        kernel,
        out_shape=jax.ShapeDtypeStruct((RC, SC, WIDTH), jnp.float32),
        scratch_shapes=[pltpu.VMEM((4, PER, 4 * GY + 16, L), jnp.float32)] + scratch,
        compiler_params=pltpu.CompilerParams(vmem_limit_bytes=16 << 20),
        cost_estimate=pl.CostEstimate(flops=1 << 20, bytes_accessed=4 << 20, transcendentals=0),
    )(*operands)


def local(a_blocks, a_cols, q_blocks, part_of, part_dest, part_pos, g_level):
    me = lax.axis_index("gy").astype(jnp.int32).reshape(1)
    g = g_level.reshape(3, B, B)
    mm = functools.partial(jnp.dot, precision=lax.Precision.HIGHEST)
    h = mm(mm(g[0], g[1]), g[2])
    send = functools.partial(lax.all_to_all, axis_name="gy", split_axis=0, concat_axis=0, tiled=True)
    mine, group = cells_of(send(fine(a_blocks, a_cols, q_blocks, part_of, part_dest, part_pos, me)))
    others = []
    for d in range(1, GX):
        others.append(lax.ppermute(group, "gx", [(i, (i + d) % GX) for i in range(GX)]))
    first = send(mine)
    total = send(merge(group, *others))
    coarse = finish(first_kernel, [], first)
    scratch = [pltpu.VMEM((B * CELLS, L), jnp.bfloat16)] * 2 + [pltpu.VMEM((B * GAP, L), jnp.float32)] * 2
    last = finish(close_kernel, scratch, total, jnp.pad(h, ((0, L - B), (0, L - B))), h.T)
    return coarse, last


def solution(mesh):
    placed = (
        P(("gx", "gy"), None, None),
        P(("gx", "gy"), None),
        P(("gx", "gy"), None),
        P(("gx", "gy"), None),
        P(("gx", "gy"), None),
        P(("gx", "gy")),
        P(),
    )
    return jax.shard_map(
        local,
        mesh=mesh,
        in_specs=placed,
        out_specs=(P(("gx", "gy"), None, None), P(("gx", "gy"), None, None)),
        check_vma=False,
    )
```

```python
import functools
import jax
import jax.numpy as jnp
from jax import lax
from jax.experimental import pallas as pl
from jax.experimental.pallas import tpu as pltpu
from jax.sharding import PartitionSpec as P

B = 96
L = 128
R = 64
KA = 8
RC = 2
SC = 8
NP = 64
CELLS = RC * SC
WIDTH = B * B
GY = 32
GX = 4
PER = B // GY
TILES = 18
ROWS_STEP = 16
STRIDE = 100
GAP = 20
M_ROWS = 512
APART = 104


def lane_iota(rows):
    return lax.broadcasted_iota(jnp.int32, (rows, L), 1)


def unpack_rows(t0, t1, t2):
    lane = lane_iota(t0.shape[0])
    r1 = jnp.where(lane < 32, pltpu.roll(t0, 32, 1), pltpu.roll(t1, 32, 1))
    r2 = jnp.where(lane < 64, pltpu.roll(t1, 64, 1), pltpu.roll(t2, 64, 1))
    return t0, r1, r2, pltpu.roll(t2, 96, 1)


def pack_rows(v0, v1, v2, v3):
    lane = lane_iota(v0.shape[0])
    s1 = pltpu.roll(v1, 96, 1)
    s2 = pltpu.roll(v2, 64, 1)
    s3 = pltpu.roll(v3, 32, 1)
    return jnp.where(lane < 96, v0, s1), jnp.where(lane < 64, s1, s2), jnp.where(lane < 32, s2, s3)


def fine_kernel(cols, part, dest, pos, me, a_hbm, q_hbm, x_hbm, a_ref, q_ref, x_ref, s_ref, q_mat, q_tr, acc, aq_ref, a_sem, q_sem, x_sem):
    steps = R // ROWS_STEP

    def fetch(step):
        at = pl.ds(pl.multiple_of(step * ROWS_STEP, ROWS_STEP), ROWS_STEP)
        return pltpu.make_async_copy(a_hbm.at[at], a_ref.at[at], a_sem.at[step])

    get_q = pltpu.make_async_copy(q_hbm, q_ref, q_sem)
    get_q.start()
    for step in range(steps):
        fetch(step).start()
    s_ref[1] = jnp.zeros((KA * STRIDE, L), jnp.float32)
    aq_ref[...] = jnp.zeros_like(aq_ref)
    acc[...] = jnp.zeros_like(acc)

    def relayout(load, slot, triples):
        for j in triples:
            rows = unpack_rows(*[load(slice(384 * j + L * u, 384 * j + L * (u + 1))).astype(jnp.float32) for u in range(3)])
            for v in range(4):
                s_ref[slot, pl.ds(4 * j + v, 8, stride=STRIDE), :] = rows[v]

    low = lane_iota(B) < B
    unit = (lane_iota(B) == lax.broadcasted_iota(jnp.int32, (B, L), 0)).astype(jnp.bfloat16)

    def spread(g, triples):
        both = slice(16 * (g // 2), 16 * (g // 2) + 16)
        relayout(lambda lanes: q_ref[both, lanes][8 * (g % 2):8 * (g % 2) + 8], g % 2, triples)

    get_q.wait()
    spread(0, range(B // 4))
    for c in range(R):
        g, k = divmod(c, 8)
        if c + 8 < R:
            spread(g + 1, range(3 * k, 3 * k + 3))
        mat = jnp.where(low, s_ref[g % 2, k * STRIDE:k * STRIDE + B, :], 0.0).astype(jnp.bfloat16)
        q_mat[c] = mat
        turned = lax.dot_general(unit, mat, (((1,), (1,)), ((), ())), preferred_element_type=jnp.float32)
        q_tr[c] = turned.astype(jnp.bfloat16)

    def first(r, slot, k):
        row = jnp.maximum(r, 0)
        for kk in (k, k + 1):
            mat = s_ref[slot, kk * STRIDE:kk * STRIDE + B, :].astype(jnp.bfloat16)
            prod = jnp.dot(mat[:, :B], q_mat[cols[kk, row]], preferred_element_type=jnp.float32)
            aq_ref[slot, k // 2, :, L * (kk - k):L * (kk - k + 1)] = prod.astype(jnp.bfloat16)

    def second(r, slot, k):
        row = jnp.maximum(r, 0)
        term = jnp.dot(q_tr[row], aq_ref[slot, k // 2], preferred_element_type=jnp.float32)
        for m in range(2):
            p = jnp.where(r < 0, NP, part[k + m, row])
            at = pl.ds(pl.multiple_of(p * APART, 8), B)
            acc[at, :] = acc[at, :] + term[:, L * m:L * (m + 1)]

    def rows_of_step(step, carry):
        fetch(step).wait()
        for ii in range(ROWS_STEP):
            r = step * ROWS_STEP + ii
            for n in range(4):
                first(r - 1, (ii + 1) % 2, 2 * n)
                relayout(lambda lanes: a_ref[r, :, lanes], ii % 2, range(6 * n, 6 * n + 6))
                second(r - 2, ii % 2, 2 * n)
        return carry

    lax.fori_loop(0, steps, rows_of_step, 0)
    for n in range(4):
        first(R - 1, (R - 1) % 2, 2 * n)
        second(R - 2, R % 2, 2 * n)
    for n in range(4):
        second(R - 1, (R - 1) % 2, 2 * n)

    row = lax.broadcasted_iota(jnp.int32, (8, L), 0)
    lane = lane_iota(8)
    base = (me[0] % 8) * 16
    codes = jnp.zeros((8, L), jnp.float32)
    for p in range(NP):
        codes = jnp.where((row == p // 16) & (lane == base + p % 16), (dest[p] * CELLS + pos[p]).astype(jnp.float32), codes)

    def leave(c):
        at = pl.ds(pl.multiple_of(c * 8, 8), 8)
        return pltpu.make_async_copy(x_ref.at[at], x_hbm.at[at], x_sem.at[c])

    def eight(c, carry):
        for n in range(8):
            w = c * 8 + n
            for a in range(PER):
                rows = [acc[pl.ds(v * 16 * APART + w * PER + a, 16, stride=APART), :] for v in range(4)]
                for u, piece in enumerate(pack_rows(*rows)):
                    for h in range(2):
                        x_ref[w, (2 * a + h) * 3 + u] = piece[8 * h:8 * h + 8]
            x_ref[w, TILES] = codes

        @pl.when(c > 0)
        def _():
            leave(c - 1).start()

        return carry

    lax.fori_loop(0, GY // 8, eight, 0)
    leave(GY // 8 - 1).start()
    for c in range(GY // 8):
        leave(c).wait()


def fine(a_blocks, a_cols, q_blocks, part_of, part_dest, part_pos, me):
    return pl.pallas_call(
        fine_kernel,
        out_shape=jax.ShapeDtypeStruct((GY, TILES + 1, 8, L), jnp.float32),
        in_specs=[pl.BlockSpec(memory_space=pltpu.SMEM)] * 5 + [pl.BlockSpec(memory_space=pltpu.HBM)] * 2,
        out_specs=pl.BlockSpec(memory_space=pltpu.HBM),
        scratch_shapes=[
            pltpu.VMEM((R, KA, WIDTH), jnp.bfloat16),
            pltpu.VMEM((R, WIDTH), jnp.bfloat16),
            pltpu.VMEM((GY, TILES + 1, 8, L), jnp.float32),
            pltpu.VMEM((2, KA * STRIDE, L), jnp.float32),
            pltpu.VMEM((R, B, L), jnp.bfloat16),
            pltpu.VMEM((R, B, B), jnp.bfloat16),
            pltpu.VMEM(((NP + 1) * APART, L), jnp.float32),
            pltpu.VMEM((2, KA // 2, B, 2 * L), jnp.bfloat16),
            pltpu.SemaphoreType.DMA((R // ROWS_STEP,)),
            pltpu.SemaphoreType.DMA,
            pltpu.SemaphoreType.DMA((GY // 8,)),
        ],
        compiler_params=pltpu.CompilerParams(vmem_limit_bytes=58 << 20),
        name="fine",
    )(a_cols.T, part_of.T, part_dest.reshape(NP), part_pos, me, a_blocks, q_blocks)


def split2(x):
    hi = x.astype(jnp.bfloat16)
    return hi, (x - hi.astype(jnp.float32)).astype(jnp.bfloat16)


def cells_kernel(y_ref, z_ref, t_ref, x_ref, m_ref, g_ref):
    wide = 2 * PER * L

    def one(s, carry):
        for a in range(PER):
            halves = [unpack_rows(*[y_ref[s, (2 * a + h) * 3 + u] for u in range(3)]) for h in range(2)]
            for v in range(4):
                hi, lo = split2(jnp.concatenate([halves[0][v], halves[1][v]], axis=0))
                at = pl.ds(pl.multiple_of(v * 512 + s * 16, 16), 16)
                x_ref[at, L * a:L * (a + 1)] = hi
                x_ref[at, L * (PER + a):L * (PER + a + 1)] = lo
        return carry

    lax.fori_loop(0, GY, one, 0, unroll=4)
    tiles = [functools.reduce(jnp.add, [y_ref[8 * o + s, TILES] for s in range(8)]) for o in range(4)]
    codes = jnp.concatenate([tiles[o][v:v + 1] for v in range(4) for o in range(4)], axis=1) - 256.0
    names = codes.astype(jnp.bfloat16)
    row = lax.broadcasted_iota(jnp.int32, (4 * L, 1), 0)
    want = ((row % L) // 4) * CELLS + 4 * (row // L) + row % 4
    want = (want.astype(jnp.float32) - 256.0).astype(jnp.bfloat16)
    one_bf, zero_bf = jnp.ones((), jnp.bfloat16), jnp.zeros((), jnp.bfloat16)
    for c in range(0, 4 * L, M_ROWS):
        table = jnp.where(want[c:c + M_ROWS] == names, one_bf, zero_bf)
        sums = jnp.dot(table, x_ref[...], preferred_element_type=jnp.float32)
        m_ref[c:c + M_ROWS, :] = sums[:, :wide // 2] + sums[:, wide // 2:]

    def fold(g, carry):
        for a in range(PER):
            for v in range(4):
                at = pl.multiple_of(L * v + 16 * g, 16)
                both = m_ref[pl.ds(at, 8), L * a:L * (a + 1)] + m_ref[pl.ds(at + 8, 8), L * a:L * (a + 1)]
                both = both + pltpu.roll(both, 4, 0)
                g_ref[a, v, pl.ds(pl.multiple_of(4 * g, 4), 4), :] = both[0:4]
        return carry

    lax.fori_loop(0, GY // 4, fold, 0, unroll=2)
    for a in range(PER):
        for u, piece in enumerate(pack_rows(*[g_ref[a, v] for v in range(4)])):
            t_ref[3 * a + u] = piece

    def pack(n, carry):
        for a in range(PER):
            rows = [m_ref[pl.ds(pl.multiple_of(L * v + 16 * n, 16), 16), L * a:L * (a + 1)] for v in range(4)]
            for u, piece in enumerate(pack_rows(*rows)):
                z_ref[3 * a + u, pl.ds(pl.multiple_of(16 * n, 16), 16), :] = piece
        return carry

    lax.fori_loop(0, L // 16, pack, 0, unroll=2)


def cells_of(received):
    return pl.pallas_call(
        cells_kernel,
        out_shape=(
            jax.ShapeDtypeStruct((3 * PER, L + 8, L), jnp.float32),
            jax.ShapeDtypeStruct((3 * PER, L // 4, L), jnp.float32),
        ),
        scratch_shapes=[
            pltpu.VMEM((4 * 512, 2 * PER * L), jnp.bfloat16),
            pltpu.VMEM((4 * L, PER * L), jnp.float32),
            pltpu.VMEM((PER, 4, L // 4, L), jnp.float32),
        ],
        compiler_params=pltpu.CompilerParams(vmem_limit_bytes=24 << 20),
        name="cells",
    )(received)


def merge_kernel(z_ref, t0, t1, t2, t3, out_ref, s_ref):
    upper = lax.broadcasted_iota(jnp.int32, (8, L), 0) < 4
    for n in range(3 * PER):
        s_ref[n, 4:L // 4 + 4, :] = (t0[n] + t1[n]) + (t2[n] + t3[n])
    for d in range(GY):
        g = d // 4
        for n in range(3 * PER):
            out_ref[d, n] = jnp.where(upper, z_ref[n, 4 * d:4 * d + 8, :], s_ref[n, 4 * g:4 * g + 8, :])


def merge(mine, parts):
    return pl.pallas_call(
        merge_kernel,
        out_shape=jax.ShapeDtypeStruct((GY, 3 * PER, 8, L), jnp.float32),
        scratch_shapes=[pltpu.VMEM((3 * PER, L // 4 + 8, L), jnp.float32)],
        compiler_params=pltpu.CompilerParams(vmem_limit_bytes=8 << 20),
        name="merge",
    )(mine, *parts)


def close_kernel(w_ref, h_ref, ht_ref, first_ref, last_ref, f_ref, hi_ref, lo_ref, r_ref, o_ref):
    upper = lax.broadcasted_iota(jnp.int32, (8, L), 0) < 4

    def spread(w, carry):
        for a in range(PER):
            rows = unpack_rows(*[w_ref[w, 3 * a + u] for u in range(3)])
            for v in range(4):
                f_ref[v, pl.ds(pl.multiple_of((w * PER + a) * 8 + 8, 8), 8), :] = rows[v]
        return carry

    lax.fori_loop(0, GY, spread, 0, unroll=4)

    def outputs(j, carry):
        lanes = [pl.ds(pl.multiple_of(384 * j + L * u, L), L) for u in range(3)]
        base = pl.multiple_of(32 * j + 8, 8)
        for half in range(RC):
            rows = [jnp.where(upper, f_ref[2 * half, pl.ds(base + 8 * v, 8), :], f_ref[2 * half + 1, pl.ds(base + 8 * v - 4, 8), :]) for v in range(4)]
            for u, piece in enumerate(pack_rows(*rows)):
                first_ref[half, :, lanes[u]] = piece
        for v in range(4):
            both = [jnp.where(upper, f_ref[2 * half, pl.ds(base + 8 * v + 4, 8), :], f_ref[2 * half + 1, pl.ds(base + 8 * v, 8), :]) for half in range(RC)]
            hi, lo = split2(jnp.concatenate(both, axis=0))
            at = pl.ds(pl.multiple_of(64 * j + 16 * v, 16), 16)
            hi_ref[at, :] = hi
            lo_ref[at, :] = lo
        return carry

    lax.fori_loop(0, B // 4, outputs, 0, unroll=2)
    h_hi, h_lo = split2(h_ref[...])
    t_hi, t_lo = split2(ht_ref[...])
    dot = functools.partial(jnp.dot, preferred_element_type=jnp.float32)
    for c in range(0, B, 16):
        at = slice(c * CELLS, (c + 16) * CELLS)
        hi, lo = hi_ref[at, :], lo_ref[at, :]
        right = dot(hi, h_hi) + (dot(lo, h_hi) + dot(hi, h_lo))
        for r in range(16):
            r_ref[(c + r) * GAP:(c + r) * GAP + CELLS, :] = right[r * CELLS:(r + 1) * CELLS]
    for c in range(0, CELLS, 2):
        pair = jnp.concatenate([r_ref[pl.ds(c + n, B, stride=GAP), :] for n in range(2)], axis=1)
        hi, lo = split2(pair)
        out = dot(t_hi, hi) + (dot(t_hi, lo) + dot(t_lo, hi))
        for n in range(2):
            o_ref[pl.ds(c + n, B, stride=GAP), :] = out[:, L * n:L * (n + 1)]
    for j in range(B // 4):
        for half in range(RC):
            rows = [o_ref[(4 * j + v) * GAP + 8 * half:(4 * j + v) * GAP + 8 * half + 8, :] for v in range(4)]
            for u, piece in enumerate(pack_rows(*rows)):
                last_ref[half, :, 384 * j + L * u:384 * j + L * (u + 1)] = piece


def close(received, h, ht):
    out = jax.ShapeDtypeStruct((RC, SC, WIDTH), jnp.float32)
    return pl.pallas_call(
        close_kernel,
        out_shape=(out, out),
        scratch_shapes=[
            pltpu.VMEM((4, B * 8 + 16, L), jnp.float32),
            pltpu.VMEM((B * CELLS, L), jnp.bfloat16),
            pltpu.VMEM((B * CELLS, L), jnp.bfloat16),
            pltpu.VMEM((B * GAP, L), jnp.float32),
            pltpu.VMEM((B * GAP, L), jnp.float32),
        ],
        compiler_params=pltpu.CompilerParams(vmem_limit_bytes=16 << 20),
        name="close",
    )(received, h, ht)


def local(a_blocks, a_cols, q_blocks, part_of, part_dest, part_pos, g_level):
    me = lax.axis_index("gy").astype(jnp.int32).reshape(1)
    g = g_level.reshape(3, B, B)
    mm = functools.partial(jnp.dot, precision=lax.Precision.HIGHEST)
    h = mm(mm(g[0], g[1]), g[2])
    slices = fine(a_blocks, a_cols, q_blocks, part_of, part_dest, part_pos, me)
    gathered = lax.all_to_all(slices, "gy", split_axis=0, concat_axis=0, tiled=True)
    mine, group = cells_of(gathered)
    others = [lax.ppermute(group, "gx", [(i, (i + d) % GX) for i in range(GX)]) for d in range(1, GX)]
    outgoing = merge(mine, [group] + others)
    back = lax.all_to_all(outgoing, "gy", split_axis=0, concat_axis=0, tiled=True)
    return close(back, jnp.pad(h, ((0, L - B), (0, L - B))), h.T)


def solution(mesh):
    placed = (
        P(("gx", "gy"), None, None),
        P(("gx", "gy"), None),
        P(("gx", "gy"), None),
        P(("gx", "gy"), None),
        P(("gx", "gy"), None),
        P(("gx", "gy")),
        P(),
    )
    return jax.shard_map(
        local,
        mesh=mesh,
        in_specs=placed,
        out_specs=(P(("gx", "gy"), None, None), P(("gx", "gy"), None, None)),
        check_vma=False,
    )
```

```python
import functools
import jax
import jax.numpy as jnp
from jax import lax
from jax.experimental import pallas as pl
from jax.experimental.pallas import tpu as pltpu
from jax.sharding import PartitionSpec as P

B = 96
L = 128
R = 64
KA = 8
RC = 2
SC = 8
NP = 64
CELLS = RC * SC
WIDTH = B * B
GY = 32
GX = 4
PER = B // GY
TILES = 18
ROWS_STEP = 16
STRIDE = 100
GAP = 20
M_ROWS = 512
APART = 104


def lane_iota(rows):
    return lax.broadcasted_iota(jnp.int32, (rows, L), 1)


def unpack_rows(t0, t1, t2):
    lane = lane_iota(t0.shape[0])
    r1 = jnp.where(lane < 32, pltpu.roll(t0, 32, 1), pltpu.roll(t1, 32, 1))
    r2 = jnp.where(lane < 64, pltpu.roll(t1, 64, 1), pltpu.roll(t2, 64, 1))
    return t0, r1, r2, pltpu.roll(t2, 96, 1)


def pack_rows(v0, v1, v2, v3):
    lane = lane_iota(v0.shape[0])
    s1 = pltpu.roll(v1, 96, 1)
    s2 = pltpu.roll(v2, 64, 1)
    s3 = pltpu.roll(v3, 32, 1)
    return jnp.where(lane < 96, v0, s1), jnp.where(lane < 64, s1, s2), jnp.where(lane < 32, s2, s3)


def fine_kernel(cols, part, dest, pos, me, a_hbm, q_hbm, x_hbm, a_ref, q_ref, x_ref, s_ref, q_mat, q_tr, acc, aq_ref, a_sem, q_sem, x_sem):
    steps = R // ROWS_STEP

    def fetch(step):
        at = pl.ds(pl.multiple_of(step * ROWS_STEP, ROWS_STEP), ROWS_STEP)
        return pltpu.make_async_copy(a_hbm.at[at], a_ref.at[at], a_sem.at[step])

    get_q = pltpu.make_async_copy(q_hbm, q_ref, q_sem)
    get_q.start()
    s_ref[1] = jnp.zeros((KA * STRIDE, L), jnp.float32)
    aq_ref[...] = jnp.zeros_like(aq_ref)
    acc[...] = jnp.zeros_like(acc)

    def relayout(load, slot, triples):
        for j in triples:
            rows = unpack_rows(*[load(slice(384 * j + L * u, 384 * j + L * (u + 1))).astype(jnp.float32) for u in range(3)])
            for v in range(4):
                s_ref[slot, pl.ds(4 * j + v, 8, stride=STRIDE), :] = rows[v]

    low = lane_iota(B) < B
    unit = (lane_iota(B) == lax.broadcasted_iota(jnp.int32, (B, L), 0)).astype(jnp.bfloat16)

    def spread(g, triples):
        both = slice(16 * (g // 2), 16 * (g // 2) + 16)
        relayout(lambda lanes: q_ref[both, lanes][8 * (g % 2):8 * (g % 2) + 8], g % 2, triples)

    get_q.wait()
    for step in range(steps):
        fetch(step).start()
    spread(0, range(B // 4))
    for c in range(R):
        g, k = divmod(c, 8)
        if c + 8 < R:
            spread(g + 1, range(3 * k, 3 * k + 3))
        mat = jnp.where(low, s_ref[g % 2, k * STRIDE:k * STRIDE + B, :], 0.0).astype(jnp.bfloat16)
        q_mat[c] = mat
        turned = lax.dot_general(unit, mat, (((1,), (1,)), ((), ())), preferred_element_type=jnp.float32)
        q_tr[c] = turned.astype(jnp.bfloat16)

    def first(r, slot, k):
        row = jnp.maximum(r, 0)
        for kk in (k, k + 1):
            mat = s_ref[slot, kk * STRIDE:kk * STRIDE + B, :].astype(jnp.bfloat16)
            prod = jnp.dot(mat[:, :B], q_mat[cols[kk, row]], preferred_element_type=jnp.float32)
            aq_ref[slot, k // 2, :, L * (kk - k):L * (kk - k + 1)] = prod.astype(jnp.bfloat16)

    def second(r, slot, k):
        row = jnp.maximum(r, 0)
        term = jnp.dot(q_tr[row], aq_ref[slot, k // 2], preferred_element_type=jnp.float32)
        for m in range(2):
            p = jnp.where(r < 0, NP, part[k + m, row])
            at = pl.ds(pl.multiple_of(p * APART, 8), B)
            acc[at, :] = acc[at, :] + term[:, L * m:L * (m + 1)]

    def rows_of_step(step, carry):
        fetch(step).wait()
        for ii in range(ROWS_STEP):
            r = step * ROWS_STEP + ii
            for n in range(4):
                first(r - 1, (ii + 1) % 2, 2 * n)
                relayout(lambda lanes: a_ref[r, :, lanes], ii % 2, range(6 * n, 6 * n + 6))
                second(r - 2, ii % 2, 2 * n)
        return carry

    lax.fori_loop(0, steps, rows_of_step, 0)
    for n in range(4):
        first(R - 1, (R - 1) % 2, 2 * n)
        second(R - 2, R % 2, 2 * n)
    for n in range(4):
        second(R - 1, (R - 1) % 2, 2 * n)

    row = lax.broadcasted_iota(jnp.int32, (8, L), 0)
    lane = lane_iota(8)
    base = (me[0] % 8) * 16
    codes = jnp.zeros((8, L), jnp.float32)
    for p in range(NP):
        codes = jnp.where((row == p // 16) & (lane == base + p % 16), (dest[p] * CELLS + pos[p]).astype(jnp.float32), codes)

    def leave(c):
        at = pl.ds(pl.multiple_of(c * 8, 8), 8)
        return pltpu.make_async_copy(x_ref.at[at], x_hbm.at[at], x_sem.at[c])

    def eight(c, carry):
        for n in range(8):
            w = c * 8 + n
            for a in range(PER):
                rows = [acc[pl.ds(v * 16 * APART + w * PER + a, 16, stride=APART), :] for v in range(4)]
                for u, piece in enumerate(pack_rows(*rows)):
                    for h in range(2):
                        x_ref[w, (2 * a + h) * 3 + u] = piece[8 * h:8 * h + 8]
            x_ref[w, TILES] = codes

        @pl.when(c > 0)
        def _():
            leave(c - 1).start()

        return carry

    lax.fori_loop(0, GY // 8, eight, 0)
    leave(GY // 8 - 1).start()
    for c in range(GY // 8):
        leave(c).wait()


def fine(a_blocks, a_cols, q_blocks, part_of, part_dest, part_pos, me):
    return pl.pallas_call(
        fine_kernel,
        out_shape=jax.ShapeDtypeStruct((GY, TILES + 1, 8, L), jnp.float32),
        in_specs=[pl.BlockSpec(memory_space=pltpu.SMEM)] * 5 + [pl.BlockSpec(memory_space=pltpu.HBM)] * 2,
        out_specs=pl.BlockSpec(memory_space=pltpu.HBM),
        scratch_shapes=[
            pltpu.VMEM((R, KA, WIDTH), jnp.bfloat16),
            pltpu.VMEM((R, WIDTH), jnp.bfloat16),
            pltpu.VMEM((GY, TILES + 1, 8, L), jnp.float32),
            pltpu.VMEM((2, KA * STRIDE, L), jnp.float32),
            pltpu.VMEM((R, B, L), jnp.bfloat16),
            pltpu.VMEM((R, B, B), jnp.bfloat16),
            pltpu.VMEM(((NP + 1) * APART, L), jnp.float32),
            pltpu.VMEM((2, KA // 2, B, 2 * L), jnp.bfloat16),
            pltpu.SemaphoreType.DMA((R // ROWS_STEP,)),
            pltpu.SemaphoreType.DMA,
            pltpu.SemaphoreType.DMA((GY // 8,)),
        ],
        compiler_params=pltpu.CompilerParams(vmem_limit_bytes=58 << 20),
        name="fine",
    )(a_cols.T, part_of.T, part_dest.reshape(NP), part_pos, me, a_blocks, q_blocks)


def split2(x):
    hi = x.astype(jnp.bfloat16)
    return hi, (x - hi.astype(jnp.float32)).astype(jnp.bfloat16)


def cells_kernel(y_ref, z_ref, t_ref, x_ref, m_ref, g_ref):
    wide = 2 * PER * L

    def one(s, carry):
        for a in range(PER):
            halves = [unpack_rows(*[y_ref[s, (2 * a + h) * 3 + u] for u in range(3)]) for h in range(2)]
            for v in range(4):
                hi, lo = split2(jnp.concatenate([halves[0][v], halves[1][v]], axis=0))
                at = pl.ds(pl.multiple_of(v * 512 + s * 16, 16), 16)
                x_ref[at, L * a:L * (a + 1)] = hi
                x_ref[at, L * (PER + a):L * (PER + a + 1)] = lo
        return carry

    lax.fori_loop(0, GY, one, 0, unroll=4)
    tiles = [functools.reduce(jnp.add, [y_ref[8 * o + s, TILES] for s in range(8)]) for o in range(4)]
    codes = jnp.concatenate([tiles[o][v:v + 1] for v in range(4) for o in range(4)], axis=1) - 256.0
    names = codes.astype(jnp.bfloat16)
    row = lax.broadcasted_iota(jnp.int32, (4 * L, 1), 0)
    want = ((row % L) // 4) * CELLS + 4 * (row // L) + row % 4
    want = (want.astype(jnp.float32) - 256.0).astype(jnp.bfloat16)
    one_bf, zero_bf = jnp.ones((), jnp.bfloat16), jnp.zeros((), jnp.bfloat16)
    for c in range(0, 4 * L, M_ROWS):
        table = jnp.where(want[c:c + M_ROWS] == names, one_bf, zero_bf)
        sums = jnp.dot(table, x_ref[...], preferred_element_type=jnp.float32)
        m_ref[c:c + M_ROWS, :] = sums[:, :wide // 2] + sums[:, wide // 2:]

    def fold(g, carry):
        for a in range(PER):
            for v in range(4):
                at = pl.multiple_of(L * v + 16 * g, 16)
                both = m_ref[pl.ds(at, 8), L * a:L * (a + 1)] + m_ref[pl.ds(at + 8, 8), L * a:L * (a + 1)]
                both = both + pltpu.roll(both, 4, 0)
                g_ref[a, v, pl.ds(pl.multiple_of(4 * g, 4), 4), :] = both[0:4]
        return carry

    lax.fori_loop(0, GY // 4, fold, 0, unroll=2)
    for a in range(PER):
        for u, piece in enumerate(pack_rows(*[g_ref[a, v] for v in range(4)])):
            t_ref[3 * a + u] = piece

    def pack(n, carry):
        for a in range(PER):
            rows = [m_ref[pl.ds(pl.multiple_of(L * v + 16 * n, 16), 16), L * a:L * (a + 1)] for v in range(4)]
            for u, piece in enumerate(pack_rows(*rows)):
                z_ref[3 * a + u, pl.ds(pl.multiple_of(16 * n, 16), 16), :] = piece
        return carry

    lax.fori_loop(0, L // 16, pack, 0, unroll=2)


def cells_of(received):
    return pl.pallas_call(
        cells_kernel,
        out_shape=(
            jax.ShapeDtypeStruct((3 * PER, L + 8, L), jnp.float32),
            jax.ShapeDtypeStruct((3 * PER, L // 4, L), jnp.float32),
        ),
        scratch_shapes=[
            pltpu.VMEM((4 * 512, 2 * PER * L), jnp.bfloat16),
            pltpu.VMEM((4 * L, PER * L), jnp.float32),
            pltpu.VMEM((PER, 4, L // 4, L), jnp.float32),
        ],
        compiler_params=pltpu.CompilerParams(vmem_limit_bytes=24 << 20),
        name="cells",
    )(received)


def merge_kernel(z_ref, t0, t1, t2, t3, out_ref, s_ref):
    upper = lax.broadcasted_iota(jnp.int32, (8, L), 0) < 4
    for n in range(3 * PER):
        s_ref[n, 4:L // 4 + 4, :] = (t0[n] + t1[n]) + (t2[n] + t3[n])
    for d in range(GY):
        g = d // 4
        for n in range(3 * PER):
            out_ref[d, n] = jnp.where(upper, z_ref[n, 4 * d:4 * d + 8, :], s_ref[n, 4 * g:4 * g + 8, :])


def merge(mine, parts):
    return pl.pallas_call(
        merge_kernel,
        out_shape=jax.ShapeDtypeStruct((GY, 3 * PER, 8, L), jnp.float32),
        scratch_shapes=[pltpu.VMEM((3 * PER, L // 4 + 8, L), jnp.float32)],
        compiler_params=pltpu.CompilerParams(vmem_limit_bytes=8 << 20),
        name="merge",
    )(mine, *parts)


def close_kernel(w_ref, h_ref, ht_ref, first_hbm, last_ref, f_ref, hi_ref, lo_ref, r_ref, o_ref, first_ref, first_sem):
    upper = lax.broadcasted_iota(jnp.int32, (8, L), 0) < 4

    def spread(n):
        for k in range(4 * PER):
            w, a = 4 * n + k // PER, k % PER
            rows = unpack_rows(*[w_ref[w, 3 * a + u] for u in range(3)])
            for v in range(4):
                f_ref[v, pl.ds(pl.multiple_of((w * PER + a) * 8 + 8, 8), 8), :] = rows[v]

    def outputs(j):
        lanes = [pl.ds(pl.multiple_of(384 * j + L * u, L), L) for u in range(3)]
        base = pl.multiple_of(32 * j + 8, 8)
        for half in range(RC):
            rows = [jnp.where(upper, f_ref[2 * half, pl.ds(base + 8 * v, 8), :], f_ref[2 * half + 1, pl.ds(base + 8 * v - 4, 8), :]) for v in range(4)]
            for u, piece in enumerate(pack_rows(*rows)):
                first_ref[half, :, lanes[u]] = piece
        for v in range(4):
            both = [jnp.where(upper, f_ref[2 * half, pl.ds(base + 8 * v + 4, 8), :], f_ref[2 * half + 1, pl.ds(base + 8 * v, 8), :]) for half in range(RC)]
            hi, lo = split2(jnp.concatenate(both, axis=0))
            at = pl.ds(pl.multiple_of(64 * j + 16 * v, 16), 16)
            hi_ref[at, :] = hi
            lo_ref[at, :] = lo

    def block(n, carry):
        for j in range(PER):
            outputs(PER * (n - 1) + j)
        spread(n)
        return carry

    spread(0)
    lax.fori_loop(1, GY // 4, block, 0)
    for j in range(B // 4 - PER, B // 4):
        outputs(j)
    leave = pltpu.make_async_copy(first_ref, first_hbm, first_sem)
    leave.start()
    h_hi, h_lo = split2(h_ref[...])
    t_hi, t_lo = split2(ht_ref[...])
    dot = functools.partial(jnp.dot, preferred_element_type=jnp.float32)
    for c in range(0, B, 16):
        at = slice(c * CELLS, (c + 16) * CELLS)
        hi, lo = hi_ref[at, :], lo_ref[at, :]
        right = dot(hi, h_hi) + (dot(lo, h_hi) + dot(hi, h_lo))
        for r in range(16):
            r_ref[(c + r) * GAP:(c + r) * GAP + CELLS, :] = right[r * CELLS:(r + 1) * CELLS]
    for c in range(0, CELLS, 2):
        pair = jnp.concatenate([r_ref[pl.ds(c + n, B, stride=GAP), :] for n in range(2)], axis=1)
        hi, lo = split2(pair)
        out = dot(t_hi, hi) + (dot(t_hi, lo) + dot(t_lo, hi))
        for n in range(2):
            o_ref[pl.ds(c + n, B, stride=GAP), :] = out[:, L * n:L * (n + 1)]
    for j in range(B // 4):
        for half in range(RC):
            rows = [o_ref[(4 * j + v) * GAP + 8 * half:(4 * j + v) * GAP + 8 * half + 8, :] for v in range(4)]
            for u, piece in enumerate(pack_rows(*rows)):
                last_ref[half, :, 384 * j + L * u:384 * j + L * (u + 1)] = piece
    leave.wait()


def close(received, h, ht):
    out = jax.ShapeDtypeStruct((RC, SC, WIDTH), jnp.float32)
    return pl.pallas_call(
        close_kernel,
        out_shape=(out, out),
        out_specs=(pl.BlockSpec(memory_space=pltpu.HBM), pl.BlockSpec(memory_space=pltpu.VMEM)),
        scratch_shapes=[
            pltpu.VMEM((4, B * 8 + 16, L), jnp.float32),
            pltpu.VMEM((B * CELLS, L), jnp.bfloat16),
            pltpu.VMEM((B * CELLS, L), jnp.bfloat16),
            pltpu.VMEM((B * GAP, L), jnp.float32),
            pltpu.VMEM((B * GAP, L), jnp.float32),
            pltpu.VMEM((RC, SC, WIDTH), jnp.float32),
            pltpu.SemaphoreType.DMA,
        ],
        compiler_params=pltpu.CompilerParams(vmem_limit_bytes=16 << 20),
        name="close",
    )(received, h, ht)


def local(a_blocks, a_cols, q_blocks, part_of, part_dest, part_pos, g_level):
    me = lax.axis_index("gy").astype(jnp.int32).reshape(1)
    g = g_level.reshape(3, B, B)
    mm = functools.partial(jnp.dot, precision=lax.Precision.HIGHEST)
    h = mm(mm(g[0], g[1]), g[2])
    slices = fine(a_blocks, a_cols, q_blocks, part_of, part_dest, part_pos, me)
    gathered = lax.all_to_all(slices, "gy", split_axis=0, concat_axis=0, tiled=True)
    mine, group = cells_of(gathered)
    others = [lax.ppermute(group, "gx", [(i, (i + d) % GX) for i in range(GX)]) for d in range(1, GX)]
    outgoing = merge(mine, [group] + others)
    back = lax.all_to_all(outgoing, "gy", split_axis=0, concat_axis=0, tiled=True)
    return close(back, jnp.pad(h, ((0, L - B), (0, L - B))), h.T)


def solution(mesh):
    placed = (
        P(("gx", "gy"), None, None),
        P(("gx", "gy"), None),
        P(("gx", "gy"), None),
        P(("gx", "gy"), None),
        P(("gx", "gy"), None),
        P(("gx", "gy")),
        P(),
    )
    return jax.shard_map(
        local,
        mesh=mesh,
        in_specs=placed,
        out_specs=(P(("gx", "gy"), None, None), P(("gx", "gy"), None, None)),
        check_vma=False,
    )
```

```python
import functools
import jax
import jax.numpy as jnp
from jax import lax
from jax.experimental import pallas as pl
from jax.experimental.pallas import tpu as pltpu
from jax.sharding import PartitionSpec as P

B = 96
L = 128
R = 64
KA = 8
RC = 2
SC = 8
NP = 64
CELLS = RC * SC
WIDTH = B * B
GY = 32
GX = 4
PER = B // GY
TILES = 18
ROWS_STEP = 16
STRIDE = 100
GAP = 20
APART = 104


def lane_iota(rows):
    return lax.broadcasted_iota(jnp.int32, (rows, L), 1)


def unpack_rows(t0, t1, t2):
    lane = lane_iota(t0.shape[0])
    r1 = jnp.where(lane < 32, pltpu.roll(t0, 32, 1), pltpu.roll(t1, 32, 1))
    r2 = jnp.where(lane < 64, pltpu.roll(t1, 64, 1), pltpu.roll(t2, 64, 1))
    return t0, r1, r2, pltpu.roll(t2, 96, 1)


def pack_rows(v0, v1, v2, v3):
    lane = lane_iota(v0.shape[0])
    s1 = pltpu.roll(v1, 96, 1)
    s2 = pltpu.roll(v2, 64, 1)
    s3 = pltpu.roll(v3, 32, 1)
    return jnp.where(lane < 96, v0, s1), jnp.where(lane < 64, s1, s2), jnp.where(lane < 32, s2, s3)


def fine_kernel(cols, part, dest, pos, me, a_hbm, q_hbm, x_hbm, a_ref, q_ref, x_ref, s_ref, q_mat, q_tr, acc, aq_ref, a_sem, q_sem, x_sem):
    steps = R // ROWS_STEP

    def fetch(step):
        at = pl.ds(pl.multiple_of(step * ROWS_STEP, ROWS_STEP), ROWS_STEP)
        return pltpu.make_async_copy(a_hbm.at[at], a_ref.at[at], a_sem.at[step])

    get_q = pltpu.make_async_copy(q_hbm, q_ref, q_sem)
    get_q.start()
    s_ref[1] = jnp.zeros((KA * STRIDE, L), jnp.float32)
    aq_ref[...] = jnp.zeros_like(aq_ref)
    acc[...] = jnp.zeros_like(acc)

    def relayout(load, slot, triples):
        for j in triples:
            rows = unpack_rows(*[load(slice(384 * j + L * u, 384 * j + L * (u + 1))).astype(jnp.float32) for u in range(3)])
            for v in range(4):
                s_ref[slot, pl.ds(4 * j + v, 8, stride=STRIDE), :] = rows[v]

    low = lane_iota(B) < B
    unit = (lane_iota(B) == lax.broadcasted_iota(jnp.int32, (B, L), 0)).astype(jnp.bfloat16)

    def spread(g, triples):
        both = slice(16 * (g // 2), 16 * (g // 2) + 16)
        relayout(lambda lanes: q_ref[both, lanes][8 * (g % 2):8 * (g % 2) + 8], g % 2, triples)

    get_q.wait()
    for step in range(steps):
        fetch(step).start()
    spread(0, range(B // 4))
    for c in range(R):
        g, k = divmod(c, 8)
        if c + 8 < R:
            spread(g + 1, range(3 * k, 3 * k + 3))
        mat = jnp.where(low, s_ref[g % 2, k * STRIDE:k * STRIDE + B, :], 0.0).astype(jnp.bfloat16)
        q_mat[c] = mat
        turned = lax.dot_general(unit, mat, (((1,), (1,)), ((), ())), preferred_element_type=jnp.float32)
        q_tr[c] = turned.astype(jnp.bfloat16)

    def first(r, slot, k):
        row = jnp.maximum(r, 0)
        for kk in (k, k + 1):
            mat = s_ref[slot, kk * STRIDE:kk * STRIDE + B, :].astype(jnp.bfloat16)
            prod = jnp.dot(mat[:, :B], q_mat[cols[kk, row]], preferred_element_type=jnp.float32)
            aq_ref[slot, k // 2, :, L * (kk - k):L * (kk - k + 1)] = prod.astype(jnp.bfloat16)

    def second(r, slot, k):
        row = jnp.maximum(r, 0)
        term = jnp.dot(q_tr[row], aq_ref[slot, k // 2], preferred_element_type=jnp.float32)
        for m in range(2):
            p = jnp.where(r < 0, NP, part[k + m, row])
            at = pl.ds(pl.multiple_of(p * APART, 8), B)
            acc[at, :] = acc[at, :] + term[:, L * m:L * (m + 1)]

    def rows_of_step(step, carry):
        fetch(step).wait()
        for ii in range(ROWS_STEP):
            r = step * ROWS_STEP + ii
            for n in range(4):
                first(r - 1, (ii + 1) % 2, 2 * n)
                relayout(lambda lanes: a_ref[r, :, lanes], ii % 2, range(6 * n, 6 * n + 6))
                second(r - 2, ii % 2, 2 * n)
        return carry

    lax.fori_loop(0, steps, rows_of_step, 0)
    for n in range(4):
        first(R - 1, (R - 1) % 2, 2 * n)
        second(R - 2, R % 2, 2 * n)
    for n in range(4):
        second(R - 1, (R - 1) % 2, 2 * n)

    row = lax.broadcasted_iota(jnp.int32, (8, L), 0)
    lane = lane_iota(8)
    base = (me[0] % 8) * 16
    codes = jnp.zeros((8, L), jnp.float32)
    for p in range(NP):
        codes = jnp.where((row == p // 16) & (lane == base + p % 16), (dest[p] * CELLS + pos[p]).astype(jnp.float32), codes)

    def leave(c):
        at = pl.ds(pl.multiple_of(c * 8, 8), 8)
        return pltpu.make_async_copy(x_ref.at[at], x_hbm.at[at], x_sem.at[c])

    def eight(c, carry):
        for n in range(8):
            w = c * 8 + n
            for a in range(PER):
                rows = [acc[pl.ds(v * 16 * APART + w * PER + a, 16, stride=APART), :] for v in range(4)]
                for u, piece in enumerate(pack_rows(*rows)):
                    for h in range(2):
                        x_ref[w, (2 * a + h) * 3 + u] = piece[8 * h:8 * h + 8]
            x_ref[w, TILES] = codes

        @pl.when(c > 0)
        def _():
            leave(c - 1).start()

        return carry

    lax.fori_loop(0, GY // 8, eight, 0)
    leave(GY // 8 - 1).start()
    for c in range(GY // 8):
        leave(c).wait()


def fine(a_blocks, a_cols, q_blocks, part_of, part_dest, part_pos, me):
    return pl.pallas_call(
        fine_kernel,
        out_shape=jax.ShapeDtypeStruct((GY, TILES + 1, 8, L), jnp.float32),
        in_specs=[pl.BlockSpec(memory_space=pltpu.SMEM)] * 5 + [pl.BlockSpec(memory_space=pltpu.HBM)] * 2,
        out_specs=pl.BlockSpec(memory_space=pltpu.HBM),
        scratch_shapes=[
            pltpu.VMEM((R, KA, WIDTH), jnp.bfloat16),
            pltpu.VMEM((R, WIDTH), jnp.bfloat16),
            pltpu.VMEM((GY, TILES + 1, 8, L), jnp.float32),
            pltpu.VMEM((2, KA * STRIDE, L), jnp.float32),
            pltpu.VMEM((R, B, L), jnp.bfloat16),
            pltpu.VMEM((R, B, B), jnp.bfloat16),
            pltpu.VMEM(((NP + 1) * APART, L), jnp.float32),
            pltpu.VMEM((2, KA // 2, B, 2 * L), jnp.bfloat16),
            pltpu.SemaphoreType.DMA((R // ROWS_STEP,)),
            pltpu.SemaphoreType.DMA,
            pltpu.SemaphoreType.DMA((GY // 8,)),
        ],
        compiler_params=pltpu.CompilerParams(vmem_limit_bytes=58 << 20),
        name="fine",
    )(a_cols.T, part_of.T, part_dest.reshape(NP), part_pos, me, a_blocks, q_blocks)


def split2(x):
    hi = x.astype(jnp.bfloat16)
    return hi, (x - hi.astype(jnp.float32)).astype(jnp.bfloat16)


def code_names(tiles, per_row):
    codes = jnp.concatenate([tiles[o][v:v + 1] for v in range(4) for o in range(4)], axis=1)
    if per_row == 4 * CELLS:
        whole = codes.astype(jnp.int32)
        codes = ((whole // per_row) * CELLS + whole % CELLS).astype(jnp.float32)
    return (codes - 256.0).astype(jnp.bfloat16)


def table_of(rows, names):
    row = lax.broadcasted_iota(jnp.int32, (rows, 1), 0)
    quarter = rows // 4
    want = ((row % quarter) // 4) * CELLS + 4 * (row // quarter) + row % 4
    want = (want.astype(jnp.float32) - 256.0).astype(jnp.bfloat16)
    return jnp.where(want == names, jnp.ones((), jnp.bfloat16), jnp.zeros((), jnp.bfloat16))


def groups_kernel(y_ref, x_ref, codes_ref, t_ref, m_ref):
    def one(s, carry):
        for a in range(PER):
            halves = [unpack_rows(*[y_ref[s, (2 * a + h) * 3 + u] for u in range(3)]) for h in range(2)]
            for v in range(4):
                hi, lo = split2(jnp.concatenate([halves[0][v], halves[1][v]], axis=0))
                at = pl.ds(pl.multiple_of(v * 512 + s * 16, 16), 16)
                x_ref[at, L * a:L * (a + 1)] = hi
                x_ref[at, L * (PER + a):L * (PER + a + 1)] = lo
        return carry

    lax.fori_loop(0, GY, one, 0, unroll=4)
    tiles = [functools.reduce(jnp.add, [y_ref[8 * o + s, TILES] for s in range(8)]) for o in range(4)]
    for o in range(4):
        codes_ref[o] = tiles[o]
    sums = jnp.dot(table_of(L, code_names(tiles, 4 * CELLS)), x_ref[...], preferred_element_type=jnp.float32)
    m_ref[...] = sums[:, :PER * L] + sums[:, PER * L:]
    for a in range(PER):
        for u, piece in enumerate(pack_rows(*[m_ref[32 * v:32 * v + 32, L * a:L * (a + 1)] for v in range(4)])):
            t_ref[3 * a + u] = piece


def groups_of(received):
    return pl.pallas_call(
        groups_kernel,
        out_shape=(
            jax.ShapeDtypeStruct((4 * 512, 2 * PER * L), jnp.bfloat16),
            jax.ShapeDtypeStruct((4, 8, L), jnp.float32),
            jax.ShapeDtypeStruct((3 * PER, L // 4, L), jnp.float32),
        ),
        scratch_shapes=[pltpu.VMEM((L, PER * L), jnp.float32)],
        compiler_params=pltpu.CompilerParams(vmem_limit_bytes=24 << 20),
        name="groups",
    )(received)


def cells_kernel(x_ref, codes_ref, z_ref, m_ref):
    names = code_names([codes_ref[o] for o in range(4)], CELLS)
    sums = jnp.dot(table_of(4 * L, names), x_ref[...], preferred_element_type=jnp.float32)
    m_ref[...] = sums[:, :PER * L] + sums[:, PER * L:]

    def pack(n, carry):
        for a in range(PER):
            rows = [m_ref[pl.ds(pl.multiple_of(L * v + 16 * n, 16), 16), L * a:L * (a + 1)] for v in range(4)]
            for u, piece in enumerate(pack_rows(*rows)):
                z_ref[3 * a + u, pl.ds(pl.multiple_of(16 * n, 16), 16), :] = piece
        return carry

    lax.fori_loop(0, L // 16, pack, 0, unroll=2)


def cells_of(x, codes):
    return pl.pallas_call(
        cells_kernel,
        out_shape=jax.ShapeDtypeStruct((3 * PER, L + 8, L), jnp.float32),
        scratch_shapes=[pltpu.VMEM((4 * L, PER * L), jnp.float32)],
        compiler_params=pltpu.CompilerParams(vmem_limit_bytes=24 << 20),
        cost_estimate=pl.CostEstimate(flops=2 * 512 * 2048 * 768, bytes_accessed=4 << 20, transcendentals=0),
        name="cells",
    )(x, codes)


def merge_kernel(z_ref, t0, t1, t2, t3, out_ref, s_ref):
    upper = lax.broadcasted_iota(jnp.int32, (8, L), 0) < 4
    for n in range(3 * PER):
        s_ref[n, 4:L // 4 + 4, :] = (t0[n] + t1[n]) + (t2[n] + t3[n])
    for d in range(GY):
        g = d // 4
        for n in range(3 * PER):
            out_ref[d, n] = jnp.where(upper, z_ref[n, 4 * d:4 * d + 8, :], s_ref[n, 4 * g:4 * g + 8, :])


def merge(mine, parts):
    return pl.pallas_call(
        merge_kernel,
        out_shape=jax.ShapeDtypeStruct((GY, 3 * PER, 8, L), jnp.float32),
        scratch_shapes=[pltpu.VMEM((3 * PER, L // 4 + 8, L), jnp.float32)],
        compiler_params=pltpu.CompilerParams(vmem_limit_bytes=8 << 20),
        name="merge",
    )(mine, *parts)


def close_kernel(w_ref, h_ref, ht_ref, first_hbm, last_ref, f_ref, hi_ref, lo_ref, r_ref, o_ref, first_ref, first_sem):
    upper = lax.broadcasted_iota(jnp.int32, (8, L), 0) < 4

    def spread(n):
        for k in range(4 * PER):
            w, a = 4 * n + k // PER, k % PER
            rows = unpack_rows(*[w_ref[w, 3 * a + u] for u in range(3)])
            for v in range(4):
                f_ref[v, pl.ds(pl.multiple_of((w * PER + a) * 8 + 8, 8), 8), :] = rows[v]

    def outputs(j):
        lanes = [pl.ds(pl.multiple_of(384 * j + L * u, L), L) for u in range(3)]
        base = pl.multiple_of(32 * j + 8, 8)
        for half in range(RC):
            rows = [jnp.where(upper, f_ref[2 * half, pl.ds(base + 8 * v, 8), :], f_ref[2 * half + 1, pl.ds(base + 8 * v - 4, 8), :]) for v in range(4)]
            for u, piece in enumerate(pack_rows(*rows)):
                first_ref[half, :, lanes[u]] = piece
        for v in range(4):
            both = [jnp.where(upper, f_ref[2 * half, pl.ds(base + 8 * v + 4, 8), :], f_ref[2 * half + 1, pl.ds(base + 8 * v, 8), :]) for half in range(RC)]
            hi, lo = split2(jnp.concatenate(both, axis=0))
            at = pl.ds(pl.multiple_of(64 * j + 16 * v, 16), 16)
            hi_ref[at, :] = hi
            lo_ref[at, :] = lo

    def block(n, carry):
        for j in range(PER):
            outputs(PER * (n - 1) + j)
        spread(n)
        return carry

    spread(0)
    lax.fori_loop(1, GY // 4, block, 0)
    for j in range(B // 4 - PER, B // 4):
        outputs(j)
    leave = pltpu.make_async_copy(first_ref, first_hbm, first_sem)
    leave.start()
    h_hi, h_lo = split2(h_ref[...])
    t_hi, t_lo = split2(ht_ref[...])
    dot = functools.partial(jnp.dot, preferred_element_type=jnp.float32)
    for c in range(0, B, 16):
        at = slice(c * CELLS, (c + 16) * CELLS)
        hi, lo = hi_ref[at, :], lo_ref[at, :]
        right = dot(hi, h_hi) + (dot(lo, h_hi) + dot(hi, h_lo))
        for r in range(16):
            r_ref[(c + r) * GAP:(c + r) * GAP + CELLS, :] = right[r * CELLS:(r + 1) * CELLS]
    for c in range(0, CELLS, 2):
        pair = jnp.concatenate([r_ref[pl.ds(c + n, B, stride=GAP), :] for n in range(2)], axis=1)
        hi, lo = split2(pair)
        out = dot(t_hi, hi) + (dot(t_hi, lo) + dot(t_lo, hi))
        for n in range(2):
            o_ref[pl.ds(c + n, B, stride=GAP), :] = out[:, L * n:L * (n + 1)]
    for j in range(B // 4):
        for half in range(RC):
            rows = [o_ref[(4 * j + v) * GAP + 8 * half:(4 * j + v) * GAP + 8 * half + 8, :] for v in range(4)]
            for u, piece in enumerate(pack_rows(*rows)):
                last_ref[half, :, 384 * j + L * u:384 * j + L * (u + 1)] = piece
    leave.wait()


def close(received, h, ht):
    out = jax.ShapeDtypeStruct((RC, SC, WIDTH), jnp.float32)
    return pl.pallas_call(
        close_kernel,
        out_shape=(out, out),
        out_specs=(pl.BlockSpec(memory_space=pltpu.HBM), pl.BlockSpec(memory_space=pltpu.VMEM)),
        scratch_shapes=[
            pltpu.VMEM((4, B * 8 + 16, L), jnp.float32),
            pltpu.VMEM((B * CELLS, L), jnp.bfloat16),
            pltpu.VMEM((B * CELLS, L), jnp.bfloat16),
            pltpu.VMEM((B * GAP, L), jnp.float32),
            pltpu.VMEM((B * GAP, L), jnp.float32),
            pltpu.VMEM((RC, SC, WIDTH), jnp.float32),
            pltpu.SemaphoreType.DMA,
        ],
        compiler_params=pltpu.CompilerParams(vmem_limit_bytes=16 << 20),
        name="close",
    )(received, h, ht)


def local(a_blocks, a_cols, q_blocks, part_of, part_dest, part_pos, g_level):
    me = lax.axis_index("gy").astype(jnp.int32).reshape(1)
    g = g_level.reshape(3, B, B)
    mm = functools.partial(jnp.dot, precision=lax.Precision.HIGHEST)
    h = mm(mm(g[0], g[1]), g[2])
    slices = fine(a_blocks, a_cols, q_blocks, part_of, part_dest, part_pos, me)
    gathered = lax.all_to_all(slices, "gy", split_axis=0, concat_axis=0, tiled=True)
    x, codes, group = groups_of(gathered)
    others = [lax.ppermute(group, "gx", [(i, (i + d) % GX) for i in range(GX)]) for d in range(1, GX)]
    mine = cells_of(x, codes)
    outgoing = merge(mine, [group] + others)
    back = lax.all_to_all(outgoing, "gy", split_axis=0, concat_axis=0, tiled=True)
    return close(back, jnp.pad(h, ((0, L - B), (0, L - B))), h.T)


def solution(mesh):
    placed = (
        P(("gx", "gy"), None, None),
        P(("gx", "gy"), None),
        P(("gx", "gy"), None),
        P(("gx", "gy"), None),
        P(("gx", "gy"), None),
        P(("gx", "gy")),
        P(),
    )
    return jax.shard_map(
        local,
        mesh=mesh,
        in_specs=placed,
        out_specs=(P(("gx", "gy"), None, None), P(("gx", "gy"), None, None)),
        check_vma=False,
    )
```

```python
import functools
import jax
import jax.numpy as jnp
from jax import lax
from jax.experimental import pallas as pl
from jax.experimental.pallas import tpu as pltpu
from jax.sharding import PartitionSpec as P

B = 96
L = 128
R = 64
KA = 8
RC = 2
SC = 8
NP = 64
CELLS = RC * SC
WIDTH = B * B
GY = 32
GX = 4
PER = B // GY
TILES = 18
ROWS_STEP = 16
STRIDE = 100
GAP = 20
APART = 104


def lane_iota(rows):
    return lax.broadcasted_iota(jnp.int32, (rows, L), 1)


def unpack_rows(t0, t1, t2):
    lane = lane_iota(t0.shape[0])
    r1 = jnp.where(lane < 32, pltpu.roll(t0, 32, 1), pltpu.roll(t1, 32, 1))
    r2 = jnp.where(lane < 64, pltpu.roll(t1, 64, 1), pltpu.roll(t2, 64, 1))
    return t0, r1, r2, pltpu.roll(t2, 96, 1)


def pack_rows(v0, v1, v2, v3):
    lane = lane_iota(v0.shape[0])
    s1 = pltpu.roll(v1, 96, 1)
    s2 = pltpu.roll(v2, 64, 1)
    s3 = pltpu.roll(v3, 32, 1)
    return jnp.where(lane < 96, v0, s1), jnp.where(lane < 64, s1, s2), jnp.where(lane < 32, s2, s3)


def fine_kernel(cols, part, dest, pos, me, a_hbm, q_hbm, x_hbm, a_ref, q_ref, x_ref, s_ref, q_mat, q_tr, acc, aq_ref, a_sem, q_sem, x_sem):
    steps = R // ROWS_STEP

    def fetch(step):
        at = pl.ds(pl.multiple_of(step * ROWS_STEP, ROWS_STEP), ROWS_STEP)
        return pltpu.make_async_copy(a_hbm.at[at], a_ref.at[at], a_sem.at[step])

    def get_q(part):
        at = slice(16 * part, 16 * part + 16)
        return pltpu.make_async_copy(q_hbm.at[at], q_ref.at[at], q_sem.at[part])

    for quarter in range(R // 16):
        get_q(quarter).start()
    s_ref[1] = jnp.zeros((KA * STRIDE, L), jnp.float32)
    aq_ref[...] = jnp.zeros_like(aq_ref)
    acc[...] = jnp.zeros_like(acc)

    def relayout(load, slot, triples):
        for j in triples:
            rows = unpack_rows(*[load(slice(384 * j + L * u, 384 * j + L * (u + 1))).astype(jnp.float32) for u in range(3)])
            for v in range(4):
                s_ref[slot, pl.ds(4 * j + v, 8, stride=STRIDE), :] = rows[v]

    low = lane_iota(B) < B
    unit = (lane_iota(B) == lax.broadcasted_iota(jnp.int32, (B, L), 0)).astype(jnp.bfloat16)

    def spread(g, triples):
        both = slice(16 * (g // 2), 16 * (g // 2) + 16)
        relayout(lambda lanes: q_ref[both, lanes][8 * (g % 2):8 * (g % 2) + 8], g % 2, triples)

    get_q(0).wait()
    spread(0, range(B // 4))
    for c in range(R):
        g, k = divmod(c, 8)
        if c % 16 == 8 and c + 8 < R:
            get_q(c // 16 + 1).wait()
            if c + 24 >= R:
                for step in range(steps):
                    fetch(step).start()
        if c + 8 < R:
            spread(g + 1, range(3 * k, 3 * k + 3))
        mat = jnp.where(low, s_ref[g % 2, k * STRIDE:k * STRIDE + B, :], 0.0).astype(jnp.bfloat16)
        q_mat[c] = mat
        turned = lax.dot_general(unit, mat, (((1,), (1,)), ((), ())), preferred_element_type=jnp.float32)
        q_tr[c] = turned.astype(jnp.bfloat16)

    def first(r, slot, k):
        row = jnp.maximum(r, 0)
        for kk in (k, k + 1):
            mat = s_ref[slot, kk * STRIDE:kk * STRIDE + B, :].astype(jnp.bfloat16)
            prod = jnp.dot(mat[:, :B], q_mat[cols[kk, row]], preferred_element_type=jnp.float32)
            aq_ref[slot, k // 2, :, L * (kk - k):L * (kk - k + 1)] = prod.astype(jnp.bfloat16)

    def second(r, slot, k):
        row = jnp.maximum(r, 0)
        term = jnp.dot(q_tr[row], aq_ref[slot, k // 2], preferred_element_type=jnp.float32)
        for m in range(2):
            p = jnp.where(r < 0, NP, part[k + m, row])
            at = pl.ds(pl.multiple_of(p * APART, 8), B)
            acc[at, :] = acc[at, :] + term[:, L * m:L * (m + 1)]

    def rows_of_step(step, carry):
        fetch(step).wait()
        for ii in range(ROWS_STEP):
            r = step * ROWS_STEP + ii
            for n in range(4):
                first(r - 1, (ii + 1) % 2, 2 * n)
                relayout(lambda lanes: a_ref[r, :, lanes], ii % 2, range(6 * n, 6 * n + 6))
                second(r - 2, ii % 2, 2 * n)
        return carry

    lax.fori_loop(0, steps, rows_of_step, 0)
    for n in range(4):
        first(R - 1, (R - 1) % 2, 2 * n)
        second(R - 2, R % 2, 2 * n)
    for n in range(4):
        second(R - 1, (R - 1) % 2, 2 * n)

    row = lax.broadcasted_iota(jnp.int32, (8, L), 0)
    lane = lane_iota(8)
    base = (me[0] % 8) * 16
    codes = jnp.zeros((8, L), jnp.float32)
    for p in range(NP):
        codes = jnp.where((row == p // 16) & (lane == base + p % 16), (dest[p] * CELLS + pos[p]).astype(jnp.float32), codes)

    def leave(c):
        at = pl.ds(pl.multiple_of(c * 8, 8), 8)
        return pltpu.make_async_copy(x_ref.at[at], x_hbm.at[at], x_sem.at[c])

    def eight(c, carry):
        for n in range(8):
            w = c * 8 + n
            for a in range(PER):
                rows = [acc[pl.ds(v * 16 * APART + w * PER + a, 16, stride=APART), :] for v in range(4)]
                for u, piece in enumerate(pack_rows(*rows)):
                    for h in range(2):
                        x_ref[w, (2 * a + h) * 3 + u] = piece[8 * h:8 * h + 8]
            x_ref[w, TILES] = codes

        @pl.when(c > 0)
        def _():
            leave(c - 1).start()

        return carry

    lax.fori_loop(0, GY // 8, eight, 0)
    leave(GY // 8 - 1).start()
    for c in range(GY // 8):
        leave(c).wait()


def fine(a_blocks, a_cols, q_blocks, part_of, part_dest, part_pos, me):
    return pl.pallas_call(
        fine_kernel,
        out_shape=jax.ShapeDtypeStruct((GY, TILES + 1, 8, L), jnp.float32),
        in_specs=[pl.BlockSpec(memory_space=pltpu.SMEM)] * 5 + [pl.BlockSpec(memory_space=pltpu.HBM)] * 2,
        out_specs=pl.BlockSpec(memory_space=pltpu.HBM),
        scratch_shapes=[
            pltpu.VMEM((R, KA, WIDTH), jnp.bfloat16),
            pltpu.VMEM((R, WIDTH), jnp.bfloat16),
            pltpu.VMEM((GY, TILES + 1, 8, L), jnp.float32),
            pltpu.VMEM((2, KA * STRIDE, L), jnp.float32),
            pltpu.VMEM((R, B, L), jnp.bfloat16),
            pltpu.VMEM((R, B, B), jnp.bfloat16),
            pltpu.VMEM(((NP + 1) * APART, L), jnp.float32),
            pltpu.VMEM((2, KA // 2, B, 2 * L), jnp.bfloat16),
            pltpu.SemaphoreType.DMA((R // ROWS_STEP,)),
            pltpu.SemaphoreType.DMA((R // 16,)),
            pltpu.SemaphoreType.DMA((GY // 8,)),
        ],
        compiler_params=pltpu.CompilerParams(vmem_limit_bytes=58 << 20),
        name="fine",
    )(a_cols.T, part_of.T, part_dest.reshape(NP), part_pos, me, a_blocks, q_blocks)


def split2(x):
    hi = x.astype(jnp.bfloat16)
    return hi, (x - hi.astype(jnp.float32)).astype(jnp.bfloat16)


def code_names(tiles, per_row):
    codes = jnp.concatenate([tiles[o][v:v + 1] for v in range(4) for o in range(4)], axis=1)
    if per_row == 4 * CELLS:
        whole = codes.astype(jnp.int32)
        codes = ((whole // per_row) * CELLS + whole % CELLS).astype(jnp.float32)
    return (codes - 256.0).astype(jnp.bfloat16)


def table_of(rows, names):
    row = lax.broadcasted_iota(jnp.int32, (rows, 1), 0)
    quarter = rows // 4
    want = ((row % quarter) // 4) * CELLS + 4 * (row // quarter) + row % 4
    want = (want.astype(jnp.float32) - 256.0).astype(jnp.bfloat16)
    return jnp.where(want == names, jnp.ones((), jnp.bfloat16), jnp.zeros((), jnp.bfloat16))


def groups_kernel(y_ref, x_ref, codes_ref, t_ref, m_ref):
    def one(s, carry):
        for a in range(PER):
            halves = [unpack_rows(*[y_ref[s, (2 * a + h) * 3 + u] for u in range(3)]) for h in range(2)]
            for v in range(4):
                hi, lo = split2(jnp.concatenate([halves[0][v], halves[1][v]], axis=0))
                at = pl.ds(pl.multiple_of(v * 512 + s * 16, 16), 16)
                x_ref[at, L * a:L * (a + 1)] = hi
                x_ref[at, L * (PER + a):L * (PER + a + 1)] = lo
        return carry

    lax.fori_loop(0, GY, one, 0, unroll=4)
    tiles = [functools.reduce(jnp.add, [y_ref[8 * o + s, TILES] for s in range(8)]) for o in range(4)]
    for o in range(4):
        codes_ref[o] = tiles[o]
    sums = jnp.dot(table_of(L, code_names(tiles, 4 * CELLS)), x_ref[...], preferred_element_type=jnp.float32)
    m_ref[...] = sums[:, :PER * L] + sums[:, PER * L:]
    for a in range(PER):
        for u, piece in enumerate(pack_rows(*[m_ref[32 * v:32 * v + 32, L * a:L * (a + 1)] for v in range(4)])):
            t_ref[3 * a + u] = piece


def groups_of(received):
    return pl.pallas_call(
        groups_kernel,
        out_shape=(
            jax.ShapeDtypeStruct((4 * 512, 2 * PER * L), jnp.bfloat16),
            jax.ShapeDtypeStruct((4, 8, L), jnp.float32),
            jax.ShapeDtypeStruct((3 * PER, L // 4, L), jnp.float32),
        ),
        scratch_shapes=[pltpu.VMEM((L, PER * L), jnp.float32)],
        compiler_params=pltpu.CompilerParams(vmem_limit_bytes=24 << 20),
        name="groups",
    )(received)


def cells_kernel(x_ref, codes_ref, z_ref, m_ref):
    names = code_names([codes_ref[o] for o in range(4)], CELLS)
    sums = jnp.dot(table_of(4 * L, names), x_ref[...], preferred_element_type=jnp.float32)
    m_ref[...] = sums[:, :PER * L] + sums[:, PER * L:]

    def pack(n, carry):
        for a in range(PER):
            rows = [m_ref[pl.ds(pl.multiple_of(L * v + 16 * n, 16), 16), L * a:L * (a + 1)] for v in range(4)]
            for u, piece in enumerate(pack_rows(*rows)):
                z_ref[3 * a + u, pl.ds(pl.multiple_of(16 * n, 16), 16), :] = piece
        return carry

    lax.fori_loop(0, L // 16, pack, 0, unroll=2)


def cells_of(x, codes):
    return pl.pallas_call(
        cells_kernel,
        out_shape=jax.ShapeDtypeStruct((3 * PER, L + 8, L), jnp.float32),
        scratch_shapes=[pltpu.VMEM((4 * L, PER * L), jnp.float32)],
        compiler_params=pltpu.CompilerParams(vmem_limit_bytes=24 << 20),
        cost_estimate=pl.CostEstimate(flops=2 * 512 * 2048 * 768, bytes_accessed=4 << 20, transcendentals=0),
        name="cells",
    )(x, codes)


def merge_kernel(z_ref, t0, t1, t2, t3, out_ref, s_ref):
    upper = lax.broadcasted_iota(jnp.int32, (8, L), 0) < 4
    for n in range(3 * PER):
        s_ref[n, 4:L // 4 + 4, :] = (t0[n] + t1[n]) + (t2[n] + t3[n])
    for d in range(GY):
        g = d // 4
        for n in range(3 * PER):
            out_ref[d, n] = jnp.where(upper, z_ref[n, 4 * d:4 * d + 8, :], s_ref[n, 4 * g:4 * g + 8, :])


def merge(mine, parts):
    return pl.pallas_call(
        merge_kernel,
        out_shape=jax.ShapeDtypeStruct((GY, 3 * PER, 8, L), jnp.float32),
        scratch_shapes=[pltpu.VMEM((3 * PER, L // 4 + 8, L), jnp.float32)],
        compiler_params=pltpu.CompilerParams(vmem_limit_bytes=8 << 20),
        name="merge",
    )(mine, *parts)


def close_kernel(w_ref, h_ref, ht_ref, first_hbm, last_ref, f_ref, hi_ref, lo_ref, r_ref, o_ref, first_ref, first_sem):
    upper = lax.broadcasted_iota(jnp.int32, (8, L), 0) < 4

    def spread(n):
        for k in range(4 * PER):
            w, a = 4 * n + k // PER, k % PER
            rows = unpack_rows(*[w_ref[w, 3 * a + u] for u in range(3)])
            for v in range(4):
                f_ref[v, pl.ds(pl.multiple_of((w * PER + a) * 8 + 8, 8), 8), :] = rows[v]

    def outputs(j):
        lanes = [pl.ds(pl.multiple_of(384 * j + L * u, L), L) for u in range(3)]
        base = pl.multiple_of(32 * j + 8, 8)
        for half in range(RC):
            rows = [jnp.where(upper, f_ref[2 * half, pl.ds(base + 8 * v, 8), :], f_ref[2 * half + 1, pl.ds(base + 8 * v - 4, 8), :]) for v in range(4)]
            for u, piece in enumerate(pack_rows(*rows)):
                first_ref[half, :, lanes[u]] = piece
        for v in range(4):
            both = [jnp.where(upper, f_ref[2 * half, pl.ds(base + 8 * v + 4, 8), :], f_ref[2 * half + 1, pl.ds(base + 8 * v, 8), :]) for half in range(RC)]
            hi, lo = split2(jnp.concatenate(both, axis=0))
            at = pl.ds(pl.multiple_of(64 * j + 16 * v, 16), 16)
            hi_ref[at, :] = hi
            lo_ref[at, :] = lo

    def block(n, carry):
        for j in range(PER):
            outputs(PER * (n - 1) + j)
        spread(n)
        return carry

    spread(0)
    lax.fori_loop(1, GY // 4, block, 0)
    for j in range(B // 4 - PER, B // 4):
        outputs(j)
    leave = pltpu.make_async_copy(first_ref, first_hbm, first_sem)
    leave.start()
    h_hi, h_lo = split2(h_ref[...])
    t_hi, t_lo = split2(ht_ref[...])
    dot = functools.partial(jnp.dot, preferred_element_type=jnp.float32)
    for c in range(0, B, 16):
        at = slice(c * CELLS, (c + 16) * CELLS)
        hi, lo = hi_ref[at, :], lo_ref[at, :]
        right = dot(hi, h_hi) + (dot(lo, h_hi) + dot(hi, h_lo))
        for r in range(16):
            r_ref[(c + r) * GAP:(c + r) * GAP + CELLS, :] = right[r * CELLS:(r + 1) * CELLS]
    for c in range(0, CELLS, 2):
        pair = jnp.concatenate([r_ref[pl.ds(c + n, B, stride=GAP), :] for n in range(2)], axis=1)
        hi, lo = split2(pair)
        out = dot(t_hi, hi) + (dot(t_hi, lo) + dot(t_lo, hi))
        for n in range(2):
            o_ref[pl.ds(c + n, B, stride=GAP), :] = out[:, L * n:L * (n + 1)]
    for j in range(B // 4):
        for half in range(RC):
            rows = [o_ref[(4 * j + v) * GAP + 8 * half:(4 * j + v) * GAP + 8 * half + 8, :] for v in range(4)]
            for u, piece in enumerate(pack_rows(*rows)):
                last_ref[half, :, 384 * j + L * u:384 * j + L * (u + 1)] = piece
    leave.wait()


def close(received, h, ht):
    out = jax.ShapeDtypeStruct((RC, SC, WIDTH), jnp.float32)
    return pl.pallas_call(
        close_kernel,
        out_shape=(out, out),
        out_specs=(pl.BlockSpec(memory_space=pltpu.HBM), pl.BlockSpec(memory_space=pltpu.VMEM)),
        scratch_shapes=[
            pltpu.VMEM((4, B * 8 + 16, L), jnp.float32),
            pltpu.VMEM((B * CELLS, L), jnp.bfloat16),
            pltpu.VMEM((B * CELLS, L), jnp.bfloat16),
            pltpu.VMEM((B * GAP, L), jnp.float32),
            pltpu.VMEM((B * GAP, L), jnp.float32),
            pltpu.VMEM((RC, SC, WIDTH), jnp.float32),
            pltpu.SemaphoreType.DMA,
        ],
        compiler_params=pltpu.CompilerParams(vmem_limit_bytes=16 << 20),
        name="close",
    )(received, h, ht)


def local(a_blocks, a_cols, q_blocks, part_of, part_dest, part_pos, g_level):
    me = lax.axis_index("gy").astype(jnp.int32).reshape(1)
    g = g_level.reshape(3, B, B)
    mm = functools.partial(jnp.dot, precision=lax.Precision.HIGHEST)
    h = mm(mm(g[0], g[1]), g[2])
    slices = fine(a_blocks, a_cols, q_blocks, part_of, part_dest, part_pos, me)
    gathered = lax.all_to_all(slices, "gy", split_axis=0, concat_axis=0, tiled=True)
    x, codes, group = groups_of(gathered)
    others = [lax.ppermute(group, "gx", [(i, (i + d) % GX) for i in range(GX)]) for d in range(1, GX)]
    mine = cells_of(x, codes)
    outgoing = merge(mine, [group] + others)
    back = lax.all_to_all(outgoing, "gy", split_axis=0, concat_axis=0, tiled=True)
    return close(back, jnp.pad(h, ((0, L - B), (0, L - B))), h.T)


def solution(mesh):
    placed = (
        P(("gx", "gy"), None, None),
        P(("gx", "gy"), None),
        P(("gx", "gy"), None),
        P(("gx", "gy"), None),
        P(("gx", "gy"), None),
        P(("gx", "gy")),
        P(),
    )
    return jax.shard_map(
        local,
        mesh=mesh,
        in_specs=placed,
        out_specs=(P(("gx", "gy"), None, None), P(("gx", "gy"), None, None)),
        check_vma=False,
    )
```
